512 devices in a mesh: slab: 16 (over y, core), tile: 32 (over x, z).
Axes of the slice: x: 4, y: 8, z: 8, core: 2. Of those that a mesh axis runs over, the one named last changes fastest.
Arguments:
- particles: float32 [8, 1048576], P(None, ('slab', 'tile')), may hold values from -6 to 6, as said below
- halo_up: int32 [512], P(('slab', 'tile')), may hold values from 0 to 15
- halo_down: int32 [512], P(('slab', 'tile')), may hold values from 0 to 15
- tile_first: int32 [16, 4096], P('slab', 'tile'), may hold values from 0 to 511, as said below
- tile_second: int32 [16, 4096], P('slab', 'tile'), may hold values from 0 to 575
- tile_live: int32 [16, 4096], P('slab', 'tile'), may hold values from 0 to 1, as said below
- step_index: int32 [1], replicated, may hold values from 0 to 63
- time_step: float32 [1], replicated, may hold values from 0.05 to 0.5
Outputs:
- rates: float32 [4, 1048576], P(None, ('slab', 'tile'))
- advanced: float32 [7, 1048576], P(None, ('slab', 'tile'))
The draws below stay inside these ranges and needn't reach their ends.
Inputs may be any that keep to these rules, and one draw needn't show every extreme that they name: `particles`: densities lie between 0.85 and 1.15, masses between 0.0002 and 0.0008, positions between 0 and 3. `tile_first`: in each slab the 16 blocks of each device of the slab are named by exactly 128 of the slab's slots. `tile_live`: in each slab exactly half of the 4096 slots are live; how many fall on one device varies.
All inputs are finite; a program needn't handle non-finite values.
Results may differ from the reference program's by a relative error of at most 0.00018.
Values sent between devices are 32-bit elements; how exact they have to be, the bound alone decides.
A program may use at most 64 MiB of HBM per device.

```python
import math
import jax
import jax.numpy as jnp
from jax import lax

PB = 128
BLK_DEV = 16
HALO_DEV = 1
TILE_DEV = 128
EXT_BLOCKS = 576
TILES_SLAB = 4096
PARTICLES = 1048576
N_SLAB = 16
N_TILE = 32
DEVICES = 512


def draw_particles(key, part):
    subkeys = jax.random.split(key, 5)
    block_count = PARTICLES // PB
    centres = jax.random.uniform(subkeys[0], (3, block_count, 1), jnp.float32, 0.0, 2.0)
    offsets = jax.random.uniform(subkeys[1], (3, block_count, PB), jnp.float32, 0.0, 1.0)
    position = (centres + offsets).reshape(3, PARTICLES)
    velocity = jnp.clip(jax.random.normal(subkeys[2], (3, PARTICLES), jnp.float32), -4.0, 4.0)
    density = jax.random.uniform(subkeys[3], (1, PARTICLES), jnp.float32, 0.9, 1.1)
    masses = jnp.exp(jax.random.uniform(subkeys[4], (1, PARTICLES), jnp.float32, math.log(0.0002), math.log(0.0008)))
    return jnp.concatenate([position, velocity, density, masses], axis=0)


def draw_tile_first(key, part):
    subkeys = jax.random.split(jax.random.fold_in(key, 29), N_SLAB + 1)
    holders = jnp.repeat(jnp.arange(N_TILE, dtype=jnp.int32), TILE_DEV)
    within = jax.random.randint(subkeys[0], (N_SLAB, TILES_SLAB), 0, BLK_DEV)
    orders = jax.vmap(lambda one_key: jax.random.permutation(one_key, TILES_SLAB))(subkeys[1:])
    return (holders[orders] * BLK_DEV + within).astype(jnp.int32)


def draw_tile_live(key, part):
    subkeys = jax.random.split(jax.random.fold_in(key, 17), 2)
    per_device = TILES_SLAB // N_TILE
    leaning = jax.random.randint(subkeys[0], (N_SLAB, N_TILE, 1), 0, 4)
    leaning = jnp.broadcast_to(leaning, (N_SLAB, N_TILE, per_device)).reshape(N_SLAB, TILES_SLAB)
    jitter = jax.random.randint(subkeys[1], (N_SLAB, TILES_SLAB), 0, 1048576)
    scores = leaning * 1048576 + jitter
    ordering = jnp.argsort(-scores, axis=1, stable=True)
    ranking = jnp.argsort(ordering, axis=1, stable=True)
    return (ranking < TILES_SLAB // 2).astype(jnp.int32)


def touch_ends(entries, own_key, smallest, top_value):
    place = [jax.random.randint(jax.random.fold_in(own_key, axis), (), 0, length) for axis, length in enumerate(entries.shape)]
    widest = entries.shape.index(max(entries.shape))
    beside = place[:widest] + [(place[widest] + 1) % entries.shape[widest]] + place[widest + 1:]
    return entries.at[tuple(place)].set(smallest).at[tuple(beside)].set(top_value)


def setup_inputs(seed: int = 0) -> dict:
    splits = jax.random.split(jax.random.key(seed), 9)
    return {
        "particles": draw_particles(jax.random.fold_in(splits[8], 71), 0),
        "halo_up": touch_ends(jax.random.randint(splits[1], (HALO_DEV * DEVICES,), 0, BLK_DEV), jax.random.fold_in(splits[1], 1), 0, BLK_DEV - 1).astype(jnp.int32),
        "halo_down": touch_ends(jax.random.randint(splits[2], (HALO_DEV * DEVICES,), 0, BLK_DEV), jax.random.fold_in(splits[2], 1), 0, BLK_DEV - 1).astype(jnp.int32),
        "tile_first": draw_tile_first(jax.random.fold_in(splits[8], 71), 0),
        "tile_second": touch_ends(jax.random.randint(splits[4], (N_SLAB, TILES_SLAB), 0, EXT_BLOCKS), jax.random.fold_in(splits[4], 1), 0, EXT_BLOCKS - 1).astype(jnp.int32),
        "tile_live": draw_tile_live(jax.random.fold_in(splits[8], 71), 0),
        "step_index": jax.random.randint(splits[6], (1,), 0, 64).astype(jnp.int32),
        "time_step": jnp.clip(jnp.exp(jax.random.uniform(splits[7], (1,), jnp.float32, math.log(0.05), math.log(0.5))), 0.05, 0.5),
    }


SMOOTHING = 1.0
KERNEL_NORM = 21.0 / (16.0 * 3.141592653589793)
SOUND_SPEED = 10.0
STIFFNESS = SOUND_SPEED * SOUND_SPEED / 7.0
VISCOSITY = 0.1
BLAST_STRENGTH = 8.0
DECAY_TIME = 8.0

def carried_fields(particles):
    density = particles[6]
    pressure = STIFFNESS * (density ** 7 - 1.0)
    return jnp.concatenate([particles[0:6], particles[7:8], (pressure / (density * density))[None], density[None]], axis=0)

def pair_terms(owned_block, neighbour):
    offsets = owned_block[0:3, :, :, None] - neighbour[0:3, :, None, :]
    dist_sq = lax.optimization_barrier(jnp.sum(offsets * offsets, axis=0))
    support = jnp.maximum(1.0 - jnp.sqrt(dist_sq) / (2.0 * SMOOTHING), 0.0)
    gradient = -5.0 * KERNEL_NORM * support ** 3 / SMOOTHING ** 5
    approach = lax.optimization_barrier(jnp.sum((owned_block[3:6, :, :, None] - neighbour[3:6, :, None, :]) * offsets, axis=0))
    masses = neighbour[6][:, None, :]
    density_rate = lax.optimization_barrier(jnp.sum(masses * approach * gradient, axis=2))
    mean_density = 0.5 * (owned_block[8][:, :, None] + neighbour[8][:, None, :])
    damping = -VISCOSITY * SOUND_SPEED * SMOOTHING * jnp.minimum(approach, 0.0) / ((dist_sq + 0.01 * SMOOTHING * SMOOTHING) * mean_density)
    pressing = -masses * (owned_block[7][:, :, None] + neighbour[7][:, None, :] + damping) * gradient
    forcing = lax.optimization_barrier(jnp.sum(pressing[None] * offsets, axis=3))
    return jnp.concatenate([density_rate[None], forcing], axis=0)

def finish(particles, tile_rates, step_index, time_step):
    step_length = time_step[0]
    elapsed = step_index[0].astype(particles.dtype) * step_length
    strength = BLAST_STRENGTH * jnp.exp(-elapsed / DECAY_TIME)
    relative = particles[0:3] + 1.0
    spread_sq = lax.optimization_barrier(jnp.sum(relative * relative, axis=0)) + 1.0
    source = strength * relative / (spread_sq * jnp.sqrt(spread_sq))
    forcing = tile_rates[1:4] + source
    rates = jnp.concatenate([tile_rates[0:1], forcing], axis=0)
    velocity = particles[3:6] + step_length * forcing
    position = particles[0:3] + step_length * velocity
    density = particles[6:7] + step_length * tile_rates[0:1]
    return (rates, jnp.concatenate([position, velocity, density], axis=0))

def slab_rates(slab_item):
    extended, first_ids, second_ids, live_flags = slab_item
    batch_size = TILE_DEV
    turn_count = first_ids.shape[0] // batch_size
    scales = live_flags.astype(extended.dtype)

    def accumulate(running, batch_item):
        owned_ids, other_ids, weights = batch_item
        owned_block = jnp.take(extended, owned_ids, axis=1)
        neighbour = jnp.take(extended, other_ids, axis=1)
        pair_sums = pair_terms(owned_block, neighbour) * weights[None, :, None]
        running = running + jax.ops.segment_sum(jnp.moveaxis(pair_sums, 1, 0), owned_ids, num_segments=BLK_DEV * N_TILE)
        return (running, None)
    initial = jnp.zeros((BLK_DEV * N_TILE, 4, PB), extended.dtype)
    running, ignored = lax.scan(accumulate, initial, (first_ids.reshape(turn_count, batch_size), second_ids.reshape(turn_count, batch_size), scales.reshape(turn_count, batch_size)))
    return jnp.transpose(running, (1, 0, 2))

def reference(particles, halo_up, halo_down, tile_first, tile_second, tile_live, step_index, time_step):
    carried = carried_fields(particles)
    blocks = carried.reshape(9, N_SLAB, N_TILE, BLK_DEV, PB)

    def chosen(indices):
        pick_index = jnp.broadcast_to(indices.astype(jnp.int32).reshape(1, N_SLAB, N_TILE, HALO_DEV, 1), (9, N_SLAB, N_TILE, HALO_DEV, PB))
        return jnp.take_along_axis(blocks, pick_index, axis=3).reshape(9, N_SLAB, N_TILE * HALO_DEV, PB)
    sent_up = chosen(halo_up)
    sent_down = chosen(halo_down)
    empty_rim = jnp.zeros((9, 1, N_TILE * HALO_DEV, PB), carried.dtype)
    from_below = jnp.concatenate([empty_rim, sent_up[:, :-1]], axis=1)
    from_above = jnp.concatenate([sent_down[:, 1:], empty_rim], axis=1)
    owned_blocks = blocks.reshape(9, N_SLAB, BLK_DEV * N_TILE, PB)
    extended = jnp.concatenate([owned_blocks, from_below, from_above], axis=2)
    extended = jnp.transpose(extended, (1, 0, 2, 3))
    slab_sums = lax.map(slab_rates, (extended, tile_first, tile_second, tile_live))
    tile_rates = jnp.transpose(slab_sums, (1, 0, 2, 3)).reshape(4, -1)
    return finish(particles, tile_rates, step_index, time_step)
```

```python
import heapq
import itertools

import jax
import jax.numpy as jnp
from jax import lax
from jax.experimental import pallas as pl
from jax.experimental.pallas import tpu as pltpu
from jax.sharding import PartitionSpec as P

PB = 128
BLK_DEV = 16
N_SLAB = 16
X, Z = 4, 8
N_TILE = X * Z
CHUNK = BLK_DEV + 2

SMOOTHING = 1.0
KERNEL_NORM = 21.0 / (16.0 * 3.141592653589793)
SOUND_SPEED = 10.0
STIFFNESS = SOUND_SPEED * SOUND_SPEED / 7.0
VISCOSITY = 0.1
BLAST_STRENGTH = 8.0
DECAY_TIME = 8.0

MESH = pl.DeviceIdType.MESH

PARTS = (
    dict(first="z", x2="+", z4="+", lo=0, hi=0, at=0.0),
    dict(first="z", x2="+", z4="+", lo=0, hi=6, at=0.1),
    dict(first="x", x2="+", z4="+", lo=6, hi=10, at=0.1),
    dict(first="z", x2="-", z4="-", lo=10, hi=15, at=0.2),
    dict(first="x", x2="-", z4="-", lo=15, hi=18, at=2.0),
)
BLOCK_US = 4096 / 46.5e3
HOP_US = 1.66


def tree(part):
    x_from = {1: (0, "x+"), 3: (0, "x-"), 2: (1, "x+") if part["x2"] == "+" else (3, "x-")}
    z_from = {1: (0, "z+"), 2: (1, "z+"), 3: (2, "z+"), 7: (0, "z-"), 6: (7, "z-"), 5: (6, "z-")}
    z_from[4] = (3, "z+") if part["z4"] == "+" else (5, "z-")
    children = {}
    for dx, dz in itertools.product(range(X), range(Z)):
        if (dx, dz) == (0, 0):
            continue
        along_z = dz != 0 if part["first"] == "x" else dx == 0
        if along_z:
            parent, way = (dx, z_from[dz][0]), z_from[dz][1]
        else:
            parent, way = (x_from[dx][0], dz), x_from[dx][1]
        children.setdefault(parent, []).append((way, (dx, dz)))
    return children


def schedule():
    trees = [tree(part) for part in PARTS]

    def depth(index, node):
        return max([0] + [1 + depth(index, child) for _, child in trees[index].get(node, [])])

    free = {"x+": 0.0, "x-": 0.0, "z+": 0.0, "z-": 0.0}
    ticket = itertools.count()
    events = [(part["at"], next(ticket), index, (0, 0)) for index, part in enumerate(PARTS)]
    heapq.heapify(events)
    steps = []
    while events:
        now, _, index, node = heapq.heappop(events)
        sends = sorted(trees[index].get(node, []), key=lambda item: -depth(index, item[1]))
        steps.append((index, node, sends))
        blocks = PARTS[index]["hi"] - PARTS[index]["lo"] or 0.5
        for way, child in sends:
            done = max(now, free[way]) + blocks * BLOCK_US
            free[way] = done
            heapq.heappush(events, (done + HOP_US, next(ticket), index, child))
    return steps


STEPS = schedule()


def gather_kernel(up_ref, down_ref, first_ref, second_ref, live_ref, mine_ref,
                  all_ref, lists_ref,
                  own, rim, tiles, own_sem, place_sem, tiles_sem, rim_send, rim_recv, send_sem, recv_sem):
    slab = lax.axis_index("slab")
    tile = lax.axis_index("tile")
    x, z = tile // Z, tile % Z
    above = lax.rem(slab + 1, N_SLAB)
    below = lax.rem(slab + N_SLAB - 1, N_SLAB)
    beside = {
        "x+": lax.rem(x + 1, X) * Z + z,
        "x-": lax.rem(x + X - 1, X) * Z + z,
        "z+": x * Z + lax.rem(z + 1, Z),
        "z-": x * Z + lax.rem(z + Z - 1, Z),
    }
    load = pltpu.make_async_copy(mine_ref, own, own_sem)
    load.start()
    barrier = pltpu.get_barrier_semaphore()
    for way in beside:
        pl.semaphore_signal(barrier, inc=1, device_id=(slab, beside[way]), device_id_type=MESH)
    pl.semaphore_signal(barrier, inc=1, device_id=(above, tile), device_id_type=MESH)
    pl.semaphore_signal(barrier, inc=1, device_id=(below, tile), device_id_type=MESH)
    tiles[0:1, :] = first_ref[...]
    tiles[1:2, :] = second_ref[...]
    tiles[2:3, :] = live_ref[...]
    tiles[3:4, :] = jnp.zeros((1, PB), jnp.int32)
    load.wait()
    rim[0] = own[up_ref[0]]
    rim[1] = own[down_ref[0]]
    place = pltpu.make_async_copy(own, all_ref.at[tile, pl.ds(0, BLK_DEV)], place_sem)
    place.start()
    mark = pltpu.make_async_copy(tiles, lists_ref.at[tile], tiles_sem)
    mark.start()
    pl.semaphore_wait(barrier, 6)

    def rim_copy(side):
        return pltpu.make_async_remote_copy(
            src_ref=rim.at[side],
            dst_ref=all_ref.at[tile, BLK_DEV + side],
            send_sem=rim_send.at[side],
            recv_sem=rim_recv.at[side],
            device_id=(above if side == 0 else below, tile),
            device_id_type=MESH,
        )

    rims = [rim_copy(0), rim_copy(1)]
    for copy in rims:
        copy.start()
    place.wait()
    mark.wait()

    def piece(index, node):
        origin = lax.rem(x + X - node[0], X) * Z + lax.rem(z + Z - node[1], Z)
        if index == 0:
            return lists_ref.at[origin]
        part = PARTS[index]
        return all_ref.at[origin, pl.ds(part["lo"], part["hi"] - part["lo"])]

    def slot(index, node):
        return index * N_TILE + node[0] * Z + node[1]

    sent = []
    for index, node, sends in STEPS:
        held = piece(index, node)
        if node != (0, 0):
            pltpu.make_async_remote_copy(
                src_ref=held,
                dst_ref=held,
                send_sem=send_sem.at[slot(index, node)],
                recv_sem=recv_sem.at[slot(index, node)],
                device_id=(slab, beside["x+"]),
                device_id_type=MESH,
            ).wait_recv()
        elif PARTS[index]["hi"] > BLK_DEV:
            for copy in rims:
                copy.wait_recv()
        for way, child in sends:
            copy = pltpu.make_async_remote_copy(
                src_ref=held,
                dst_ref=held,
                send_sem=send_sem.at[slot(index, child)],
                recv_sem=recv_sem.at[slot(index, child)],
                device_id=(slab, beside[way]),
                device_id_type=MESH,
            )
            copy.start()
            sent.append(copy)
    for copy in rims:
        copy.wait_send()
    for copy in sent:
        copy.wait_send()


def gather(halo_up, halo_down, tile_first, tile_second, tile_live, mine):
    smem = pl.BlockSpec(memory_space=pltpu.SMEM)
    vmem = pl.BlockSpec(memory_space=pltpu.VMEM)
    anywhere = pl.BlockSpec(memory_space=pl.ANY)
    slots = len(PARTS) * N_TILE
    return pl.pallas_call(
        gather_kernel,
        out_shape=(
            jax.ShapeDtypeStruct((N_TILE, CHUNK, 8, PB), jnp.float32),
            jax.ShapeDtypeStruct((N_TILE, 4, PB), jnp.int32),
        ),
        in_specs=[smem, smem, vmem, vmem, vmem, anywhere],
        out_specs=(anywhere, anywhere),
        scratch_shapes=[
            pltpu.VMEM((BLK_DEV, 8, PB), jnp.float32),
            pltpu.VMEM((2, 8, PB), jnp.float32),
            pltpu.VMEM((4, PB), jnp.int32),
            pltpu.SemaphoreType.DMA,
            pltpu.SemaphoreType.DMA,
            pltpu.SemaphoreType.DMA,
            pltpu.SemaphoreType.DMA((2,)),
            pltpu.SemaphoreType.DMA((2,)),
            pltpu.SemaphoreType.DMA((slots,)),
            pltpu.SemaphoreType.DMA((slots,)),
        ],
        compiler_params=pltpu.CompilerParams(collective_id=0, has_side_effects=True, vmem_limit_bytes=4 * 2**20),
        name="gather_blocks",
    )(halo_up, halo_down, tile_first, tile_second, tile_live, mine)


def iota(shape, axis):
    return lax.broadcasted_iota(jnp.int32, shape, axis)


def choose_tiles(lists, slab, tile):
    first, second, live = lists[:, 0, :], lists[:, 1, :], lists[:, 2, :]
    missing = ((slab == 0) & (second >= 512) & (second < 544)) | ((slab == N_SLAB - 1) & (second >= 544))
    wanted = ((first >> 4) == tile) & (live == 1) & jnp.logical_not(missing)
    source = jnp.where(
        second < 512,
        (second >> 4) * CHUNK + (second & 15),
        ((second - 512) & 31) * CHUNK + BLK_DEV + ((second - 512) >> 5),
    )
    code = ((first & 15) * 1024 + source).astype(jnp.float32)
    ones = jnp.where(wanted, 1.0, 0.0)
    upto = (iota((PB, PB), 0) <= iota((PB, PB), 1)).astype(jnp.float32)
    within = jnp.dot(ones, upto, preferred_element_type=jnp.float32)
    earlier = (iota((N_TILE, N_TILE), 1) < iota((N_TILE, N_TILE), 0)).astype(jnp.float32)
    before = jnp.dot(earlier, within, preferred_element_type=jnp.float32)[:, PB - 1 :]
    place = jnp.where(wanted, (before + within).astype(jnp.int32) - 1, -1)
    target = iota((PB, PB), 0)
    chosen = jnp.zeros((PB, PB), jnp.float32)
    for row in range(N_TILE):
        chosen = chosen + jnp.where(place[row : row + 1, :] == target, code[row : row + 1, :], 0.0)
    codes = lax.dot_general(
        jnp.ones((8, PB), jnp.float32), chosen, (((1,), (1,)), ((), ())),
        precision=lax.Precision.HIGHEST, preferred_element_type=jnp.float32,
    )
    count = jnp.sum(before[N_TILE - 1 :, :] + within[N_TILE - 1 :, PB - 1 :])
    return jnp.where(iota((8, PB), 0) == 0, codes, count).astype(jnp.int32)


def rates_kernel(step_ref, length_ref, mine_ref, lists_ref, all_ref, rates_ref, ahead_ref,
                 own, total, codes, plan, plan_sem):
    slab = lax.axis_index("slab")
    tile = lax.axis_index("tile")
    codes[...] = choose_tiles(lists_ref[...], slab, tile)
    copy = pltpu.make_async_copy(codes, plan, plan_sem)
    copy.start()
    total[...] = jnp.zeros_like(total)
    for block in range(BLK_DEV):
        fields = mine_ref[block]
        density = fields[6:7]
        squared = density * density
        pressure = STIFFNESS * (squared * squared * squared * density - 1.0)
        own[block] = jnp.concatenate([fields[0:6], density, pressure / squared], axis=0)
    copy.wait()

    def one_tile(k, carry):
        code = plan[0, k]
        a = code >> 10
        fields = all_ref[code & 1023]
        density = fields[6:7]
        squared = density * density
        pressure = STIFFNESS * (squared * squared * squared * density - 1.0)
        scaled_mass = fields[7:8] * (5.0 * KERNEL_NORM / 8.0)
        table = jnp.concatenate(
            [fields[0:7], scaled_mass, pressure / squared, jnp.zeros((7, PB), jnp.float32)], axis=0
        ).T
        ax, ay, az, au, av, aw, arho, aq = (
            jnp.broadcast_to(own[a, pl.ds(row, 1), :], (8, PB)) for row in range(8)
        )
        sums = [jnp.zeros((8, PB), jnp.float32)] * 4
        for group in range(PB // 8):
            rows = table[group * 8 : group * 8 + 8]
            bx, by, bz, bu, bv, bw, brho, bm, bq = (
                jnp.broadcast_to(rows[:, column : column + 1], (8, PB)) for column in range(9)
            )
            dx, dy, dz = ax - bx, ay - by, az - bz
            dist_sq = dx * dx + dy * dy + dz * dz
            dist = jnp.sqrt(dist_sq)
            reach = jnp.maximum(2.0 - dist, 0.0)
            weight = bm * (reach * reach * reach)
            approach = (au - bu) * dx + (av - bv) * dy + (aw - bw) * dz
            damping = -2.0 * jnp.minimum(approach, 0.0) / ((dist_sq + 0.01) * (arho + brho))
            pressing = (aq + bq + damping) * weight
            sums[0] = sums[0] - approach * weight
            sums[1] = sums[1] + pressing * dx
            sums[2] = sums[2] + pressing * dy
            sums[3] = sums[3] + pressing * dz
        for row in range(4):
            total[a, row] += sums[row]
        return carry

    lax.fori_loop(0, plan[1, 0], one_tile, 0)
    length = length_ref[0]
    elapsed = step_ref[0].astype(jnp.float32) * length
    strength = BLAST_STRENGTH * jnp.exp(jnp.full((1, PB), -elapsed / DECAY_TIME, jnp.float32))
    for block in range(BLK_DEV):
        fields = mine_ref[block]
        columns = pl.ds(block * PB, PB)
        sums = jnp.concatenate(
            [jnp.sum(total[block, row], axis=0, keepdims=True) for row in range(4)], axis=0
        )
        relative = fields[0:3] + 1.0
        spread_sq = jnp.sum(relative * relative, axis=0, keepdims=True) + 1.0
        source = strength * relative / (spread_sq * jnp.sqrt(spread_sq))
        forcing = sums[1:4] + source
        velocity = fields[3:6] + length * forcing
        position = fields[0:3] + length * velocity
        density = fields[6:7] + length * sums[0:1]
        rates_ref[:, columns] = jnp.concatenate([sums[0:1], forcing], axis=0)
        ahead_ref[:, columns] = jnp.concatenate([position, velocity, density], axis=0)


def rates_of(step_index, time_step, mine, lists, gathered):
    smem = pl.BlockSpec(memory_space=pltpu.SMEM)
    vmem = pl.BlockSpec(memory_space=pltpu.VMEM)
    return pl.pallas_call(
        rates_kernel,
        out_shape=(
            jax.ShapeDtypeStruct((4, BLK_DEV * PB), jnp.float32),
            jax.ShapeDtypeStruct((7, BLK_DEV * PB), jnp.float32),
        ),
        in_specs=[smem, smem, vmem, vmem, vmem],
        out_specs=(vmem, vmem),
        scratch_shapes=[
            pltpu.VMEM((BLK_DEV, 8, PB), jnp.float32),
            pltpu.VMEM((BLK_DEV, 4, 8, PB), jnp.float32),
            pltpu.VMEM((8, PB), jnp.int32),
            pltpu.SMEM((8, PB), jnp.int32),
            pltpu.SemaphoreType.DMA,
        ],
        compiler_params=pltpu.CompilerParams(vmem_limit_bytes=16 * 2**20),
        name="tile_rates",
    )(step_index, time_step, mine, lists, gathered)


def on_device(particles, halo_up, halo_down, tile_first, tile_second, tile_live, step_index, time_step):
    mine = jnp.transpose(particles.reshape(8, BLK_DEV, PB), (1, 0, 2))
    gathered, lists = gather(halo_up, halo_down, tile_first, tile_second, tile_live, mine)
    return rates_of(step_index, time_step, mine, lists, gathered.reshape(N_TILE * CHUNK, 8, PB))


def solution(mesh):
    placed = (
        P(None, ("slab", "tile")),
        P(("slab", "tile")),
        P(("slab", "tile")),
        P("slab", "tile"),
        P("slab", "tile"),
        P("slab", "tile"),
        P(),
        P(),
    )
    return jax.shard_map(
        on_device,
        mesh=mesh,
        in_specs=placed,
        out_specs=(P(None, ("slab", "tile")), P(None, ("slab", "tile"))),
        check_vma=False,
    )
```

```python
import heapq
import itertools

import jax
import jax.numpy as jnp
from jax import lax
from jax.experimental import pallas as pl
from jax.experimental.pallas import tpu as pltpu
from jax.sharding import PartitionSpec as P

PB = 128
BLK_DEV = 16
N_SLAB = 16
X, Z = 4, 8
N_TILE = X * Z
CHUNK = BLK_DEV + 2

SMOOTHING = 1.0
KERNEL_NORM = 21.0 / (16.0 * 3.141592653589793)
SOUND_SPEED = 10.0
STIFFNESS = SOUND_SPEED * SOUND_SPEED / 7.0
VISCOSITY = 0.1
BLAST_STRENGTH = 8.0
DECAY_TIME = 8.0

MESH = pl.DeviceIdType.MESH

PARTS = (
    dict(first="z", x2="+", z4="+", lo=0, hi=0, at=0.0),
    dict(first="z", x2="+", z4="+", lo=0, hi=6, at=0.1),
    dict(first="x", x2="+", z4="+", lo=6, hi=10, at=0.1),
    dict(first="z", x2="-", z4="-", lo=10, hi=15, at=0.2),
    dict(first="x", x2="-", z4="-", lo=15, hi=18, at=2.0),
)
BLOCK_US = 4096 / 46.5e3
HOP_US = 1.66


def tree(part):
    x_from = {1: (0, "x+"), 3: (0, "x-"), 2: (1, "x+") if part["x2"] == "+" else (3, "x-")}
    z_from = {1: (0, "z+"), 2: (1, "z+"), 3: (2, "z+"), 7: (0, "z-"), 6: (7, "z-"), 5: (6, "z-")}
    z_from[4] = (3, "z+") if part["z4"] == "+" else (5, "z-")
    children = {}
    for dx, dz in itertools.product(range(X), range(Z)):
        if (dx, dz) == (0, 0):
            continue
        along_z = dz != 0 if part["first"] == "x" else dx == 0
        if along_z:
            parent, way = (dx, z_from[dz][0]), z_from[dz][1]
        else:
            parent, way = (x_from[dx][0], dz), x_from[dx][1]
        children.setdefault(parent, []).append((way, (dx, dz)))
    return children


def schedule():
    trees = [tree(part) for part in PARTS]

    def depth(index, node):
        return max([0] + [1 + depth(index, child) for _, child in trees[index].get(node, [])])

    free = {"x+": 0.0, "x-": 0.0, "z+": 0.0, "z-": 0.0}
    ticket = itertools.count()
    events = [(part["at"], next(ticket), index, (0, 0)) for index, part in enumerate(PARTS)]
    heapq.heapify(events)
    steps = []
    while events:
        now, _, index, node = heapq.heappop(events)
        sends = sorted(trees[index].get(node, []), key=lambda item: -depth(index, item[1]))
        steps.append((index, node, sends))
        blocks = PARTS[index]["hi"] - PARTS[index]["lo"] or 0.5
        for way, child in sends:
            done = max(now, free[way]) + blocks * BLOCK_US
            free[way] = done
            heapq.heappush(events, (done + HOP_US, next(ticket), index, child))
    return steps


STEPS = schedule()


def gather_kernel(up_ref, down_ref, first_ref, second_ref, live_ref, mine_ref,
                  all_ref, lists_ref,
                  own, rim, slots, tiles, slots_sem, own_sem, place_sem, tiles_sem, rim_send, rim_recv, send_sem, recv_sem):
    slab = lax.axis_index("slab")
    tile = lax.axis_index("tile")
    x, z = tile // Z, tile % Z
    above = lax.rem(slab + 1, N_SLAB)
    below = lax.rem(slab + N_SLAB - 1, N_SLAB)
    beside = {
        "x+": lax.rem(x + 1, X) * Z + z,
        "x-": lax.rem(x + X - 1, X) * Z + z,
        "z+": x * Z + lax.rem(z + 1, Z),
        "z-": x * Z + lax.rem(z + Z - 1, Z),
    }
    load = pltpu.make_async_copy(mine_ref, own, own_sem)
    load.start()
    fetch = [
        pltpu.make_async_copy(ref, slots.at[place], slots_sem.at[place])
        for place, ref in enumerate((first_ref, second_ref, live_ref))
    ]
    for copy in fetch:
        copy.start()
    barrier = pltpu.get_barrier_semaphore()
    for way in beside:
        pl.semaphore_signal(barrier, inc=1, device_id=(slab, beside[way]), device_id_type=MESH)
    pl.semaphore_signal(barrier, inc=1, device_id=(above, tile), device_id_type=MESH)
    pl.semaphore_signal(barrier, inc=1, device_id=(below, tile), device_id_type=MESH)
    for copy in fetch:
        copy.wait()
    tiles[...] = jnp.concatenate([slots[0], slots[1], slots[2], jnp.zeros((1, PB), jnp.int32)], axis=0)
    load.wait()
    rim[0] = own[up_ref[0]]
    rim[1] = own[down_ref[0]]
    place = pltpu.make_async_copy(own, all_ref.at[tile, pl.ds(0, BLK_DEV)], place_sem)
    place.start()
    mark = pltpu.make_async_copy(tiles, lists_ref.at[tile], tiles_sem)
    mark.start()
    pl.semaphore_wait(barrier, 6)

    def rim_copy(side):
        return pltpu.make_async_remote_copy(
            src_ref=rim.at[side],
            dst_ref=all_ref.at[tile, BLK_DEV + side],
            send_sem=rim_send.at[side],
            recv_sem=rim_recv.at[side],
            device_id=(above if side == 0 else below, tile),
            device_id_type=MESH,
        )

    rims = [rim_copy(0), rim_copy(1)]
    for copy in rims:
        copy.start()
    place.wait()
    mark.wait()

    def piece(index, node):
        origin = lax.rem(x + X - node[0], X) * Z + lax.rem(z + Z - node[1], Z)
        if index == 0:
            return lists_ref.at[origin]
        part = PARTS[index]
        return all_ref.at[origin, pl.ds(part["lo"], part["hi"] - part["lo"])]

    def slot(index, node):
        return index * N_TILE + node[0] * Z + node[1]

    sent = []
    for index, node, sends in STEPS:
        held = piece(index, node)
        if node != (0, 0):
            pltpu.make_async_remote_copy(
                src_ref=held,
                dst_ref=held,
                send_sem=send_sem.at[slot(index, node)],
                recv_sem=recv_sem.at[slot(index, node)],
                device_id=(slab, beside["x+"]),
                device_id_type=MESH,
            ).wait_recv()
        elif PARTS[index]["hi"] > BLK_DEV:
            for copy in rims:
                copy.wait_recv()
        for way, child in sends:
            copy = pltpu.make_async_remote_copy(
                src_ref=held,
                dst_ref=held,
                send_sem=send_sem.at[slot(index, child)],
                recv_sem=recv_sem.at[slot(index, child)],
                device_id=(slab, beside[way]),
                device_id_type=MESH,
            )
            copy.start()
            sent.append(copy)
    for copy in rims:
        copy.wait_send()
    for copy in sent:
        copy.wait_send()


def gather(halo_up, halo_down, tile_first, tile_second, tile_live, mine):
    smem = pl.BlockSpec(memory_space=pltpu.SMEM)
    hbm = pl.BlockSpec(memory_space=pltpu.HBM)
    anywhere = pl.BlockSpec(memory_space=pl.ANY)
    slots = len(PARTS) * N_TILE
    return pl.pallas_call(
        gather_kernel,
        out_shape=(
            jax.ShapeDtypeStruct((N_TILE, CHUNK, 8, PB), jnp.float32),
            jax.ShapeDtypeStruct((N_TILE, 4, PB), jnp.int32),
        ),
        in_specs=[smem, smem, hbm, hbm, hbm, hbm],
        out_specs=(anywhere, anywhere),
        scratch_shapes=[
            pltpu.VMEM((BLK_DEV, 8, PB), jnp.float32),
            pltpu.VMEM((2, 8, PB), jnp.float32),
            pltpu.VMEM((3, 1, PB), jnp.int32),
            pltpu.VMEM((4, PB), jnp.int32),
            pltpu.SemaphoreType.DMA((3,)),
            pltpu.SemaphoreType.DMA,
            pltpu.SemaphoreType.DMA,
            pltpu.SemaphoreType.DMA,
            pltpu.SemaphoreType.DMA((2,)),
            pltpu.SemaphoreType.DMA((2,)),
            pltpu.SemaphoreType.DMA((slots,)),
            pltpu.SemaphoreType.DMA((slots,)),
        ],
        compiler_params=pltpu.CompilerParams(collective_id=0, has_side_effects=True, vmem_limit_bytes=4 * 2**20),
        name="gather_blocks",
    )(halo_up, halo_down, tile_first, tile_second, tile_live, mine)


def iota(shape, axis):
    return lax.broadcasted_iota(jnp.int32, shape, axis)


def choose_tiles(lists, slab, tile):
    first, second, live = lists[:, 0, :], lists[:, 1, :], lists[:, 2, :]
    missing = ((slab == 0) & (second >= 512) & (second < 544)) | ((slab == N_SLAB - 1) & (second >= 544))
    wanted = ((first >> 4) == tile) & (live == 1) & jnp.logical_not(missing)
    source = jnp.where(
        second < 512,
        (second >> 4) * CHUNK + (second & 15),
        ((second - 512) & 31) * CHUNK + BLK_DEV + ((second - 512) >> 5),
    )
    code = ((first & 15) * 1024 + source).astype(jnp.float32)
    ones = jnp.where(wanted, 1.0, 0.0)
    upto = (iota((PB, PB), 0) <= iota((PB, PB), 1)).astype(jnp.float32)
    within = jnp.dot(ones, upto, preferred_element_type=jnp.float32)
    earlier = (iota((N_TILE, N_TILE), 1) < iota((N_TILE, N_TILE), 0)).astype(jnp.float32)
    before = jnp.dot(earlier, within, preferred_element_type=jnp.float32)[:, PB - 1 :]
    place = jnp.where(wanted, (before + within).astype(jnp.int32) - 1, -1)
    target = iota((PB, PB), 0)
    chosen = jnp.zeros((PB, PB), jnp.float32)
    for row in range(N_TILE):
        chosen = chosen + jnp.where(place[row : row + 1, :] == target, code[row : row + 1, :], 0.0)
    codes = lax.dot_general(
        jnp.ones((8, PB), jnp.float32), chosen, (((1,), (1,)), ((), ())),
        precision=lax.Precision.HIGHEST, preferred_element_type=jnp.float32,
    )
    count = jnp.sum(before[N_TILE - 1 :, :] + within[N_TILE - 1 :, PB - 1 :])
    return jnp.where(iota((8, PB), 0) == 0, codes, count).astype(jnp.int32)


def shifted(rows, up):
    return pltpu.roll(rows, (8 - up) % 8, 0)


def parts_of(value):
    high = value.astype(jnp.bfloat16).astype(jnp.float32)
    rest = value - high
    middle = rest.astype(jnp.bfloat16).astype(jnp.float32)
    return high, middle, rest - middle


def squares_and_products(centred):
    squares = centred * centred
    products = centred * shifted(centred, 3)
    return (
        squares + shifted(squares, 1) + shifted(squares, 2),
        products + shifted(products, 1) + shifted(products, 2),
    )


def pressure_term(density):
    squared = density * density
    return STIFFNESS * (squared * squared * squared * density - 1.0) / squared


def receiver(fields, row):
    centre = jnp.where(row < 6, jnp.broadcast_to(fields[:, 0:1], (8, PB)), 0.0)
    centred = fields - centre
    squares, products = squares_and_products(centred)
    plain = jnp.where(row < 6, centred, jnp.where(row == 6, 1.0, 0.0))
    high, middle, low = parts_of(plain)
    extra = jnp.zeros((8, PB), jnp.float32)
    for place, value in enumerate(parts_of(squares) + parts_of(products)):
        extra = jnp.where(row == place, value if place == 0 else shifted(value, 8 - place), extra)
    pressure = pressure_term(fields)
    columns = jnp.where(row == 0, shifted(pressure, 6), jnp.where(row == 1, shifted(-0.5 * fields, 5), 0.0))
    return centre, jnp.concatenate([high, high, middle, middle, high, low, extra, columns], axis=0).T


def actor_side(centred, row):
    squares, products = squares_and_products(centred)
    for_square = jnp.where(row < 3, -2.0 * centred, jnp.where(row == 6, shifted(squares, 2), 0.0))
    for_approach = jnp.where(
        row < 3, -shifted(centred, 3), jnp.where(row < 6, -shifted(centred, 5), jnp.where(row == 6, shifted(products, 2), 0.0))
    )
    sides = []
    for value, ones in ((for_square, row < 3), (for_approach, (row >= 3) & (row < 6))):
        high, middle, low = parts_of(value)
        extra = jnp.where(ones, 1.0, 0.0)
        sides.append(
            jnp.concatenate([high, middle, high, middle, low, high, extra, jnp.zeros((8, PB), jnp.float32)], axis=0)
        )
    return jnp.concatenate(sides, axis=1).astype(jnp.bfloat16)


NO_TILE = BLK_DEV * 1024
TOGETHER = 2


def rates_kernel(step_ref, length_ref, lists_ref, all_ref, rates_ref, ahead_ref,
                 centre, left, push, rho, total, codes, right, squares, factor, moment, plan, plan_sem):
    slab = lax.axis_index("slab")
    tile = lax.axis_index("tile")
    row = iota((8, PB), 0)
    codes[...] = choose_tiles(lists_ref[...], slab, tile)
    copy = pltpu.make_async_copy(codes, plan, plan_sem)
    copy.start()
    total[...] = jnp.zeros_like(total)

    def one_block(block, carry):
        middle, side = receiver(all_ref[tile * CHUNK + block], row)
        centre[block] = middle
        left[block] = side.astype(jnp.bfloat16)
        push[block] = jnp.broadcast_to(side[:, 56:57], (PB, PB))
        rho[block] = jnp.broadcast_to(side[:, 57:58], (PB, PB))
        return carry

    lax.fori_loop(0, BLK_DEV, one_block, 0)
    copy.wait()
    number = plan[1, 0]

    def code_of(k):
        code = plan[0, jnp.clip(k, 0, PB - 1)]
        return jnp.where((k >= 0) & (k < number), code, NO_TILE)

    def prepare(k, slot):
        code = code_of(k)
        right[slot] = actor_side(all_ref[code & 1023] - centre[code >> 10], row)

    def first_product(k, slot):
        squares[slot] = jnp.dot(left[code_of(k) >> 10], right[slot], preferred_element_type=jnp.float32)

    def elementwise(k, slot):
        code = code_of(k)
        a = code >> 10
        fields = all_ref[code & 1023]
        centred = fields - centre[a]
        act_push = jnp.broadcast_to(pressure_term(fields)[6:7], (16, PB))
        act_rho = jnp.broadcast_to(-0.5 * fields[6:7], (16, PB))
        mass = jnp.broadcast_to(fields[7:8] * (5.0 * KERNEL_NORM / 8.0), (8, PB))
        weighted = jnp.where(row == 0, 1.0, shifted(centred, 7)) * mass
        high = weighted.astype(jnp.bfloat16).astype(jnp.float32)
        both = jnp.where(row < 4, high, shifted(weighted - high, 4))
        both = jnp.concatenate([both, jnp.zeros((8, PB), jnp.float32)], axis=0).astype(jnp.bfloat16)
        moment[slot] = jnp.concatenate([both, both], axis=1)
        for low in range(0, PB, 16):
            rows = pl.ds(low, 16)
            dist_sq = jnp.maximum(squares[slot, rows, 0:PB], 1e-30)
            approach = squares[slot, rows, PB : 2 * PB]
            reach = jnp.maximum(2.0 - dist_sq * lax.rsqrt(dist_sq), 0.0)
            weight = reach * reach * reach
            growth = approach * weight
            damping = jnp.minimum(approach, 0.0) / ((dist_sq + 0.01) * (rho[a, rows] + act_rho))
            pressing = (push[a, rows] + act_push + damping) * weight
            for place, value in ((0, pressing), (PB, growth)):
                high = value.astype(jnp.bfloat16)
                factor[slot, pl.ds(place + low, 16), 0:PB] = high
                factor[slot, pl.ds(place + low, 16), PB : 2 * PB] = (value - high.astype(jnp.float32)).astype(jnp.bfloat16)

    def second_product(k, slot):
        a = code_of(k) >> 10
        sums = lax.dot_general(
            moment[slot], factor[slot], (((1,), (1,)), ((), ())), preferred_element_type=jnp.float32
        )
        total[a, 0] += sums[0:8, 0:PB]
        total[a, 1] += sums[0:8, PB : 2 * PB]

    def one_step(step, carry):
        for slot in range(TOGETHER):
            second_product(TOGETHER * (step - 3) + slot, slot)
        for slot in range(TOGETHER):
            elementwise(TOGETHER * (step - 2) + slot, slot)
        for slot in range(TOGETHER):
            first_product(TOGETHER * (step - 1) + slot, slot)
        for slot in range(TOGETHER):
            prepare(TOGETHER * step + slot, slot)
        return carry

    lax.fori_loop(0, (number + 4 * TOGETHER - 1) // TOGETHER, one_step, 0)
    length = length_ref[0]
    elapsed = step_ref[0].astype(jnp.float32) * length
    strength = BLAST_STRENGTH * jnp.exp(jnp.full((1, PB), -elapsed / DECAY_TIME, jnp.float32))
    for block in range(BLK_DEV):
        fields = all_ref[tile * CHUNK + block]
        columns = pl.ds(block * PB, PB)
        moments = total[block, 0, 0:4] + total[block, 0, 4:8]
        growth = -(total[block, 1, 0:1] + total[block, 1, 4:5])
        relative = fields[0:3] + 1.0
        spread_sq = jnp.sum(relative * relative, axis=0, keepdims=True) + 1.0
        source = strength * relative / (spread_sq * jnp.sqrt(spread_sq))
        pushed = (fields - centre[block])[0:3] * moments[0:1] - moments[1:4]
        forcing = pushed + source
        velocity = fields[3:6] + length * forcing
        position = fields[0:3] + length * velocity
        density = fields[6:7] + length * growth
        rates_ref[:, columns] = jnp.concatenate([growth, forcing], axis=0)
        ahead_ref[:, columns] = jnp.concatenate([position, velocity, density], axis=0)


def rates_of(step_index, time_step, lists, gathered):
    smem = pl.BlockSpec(memory_space=pltpu.SMEM)
    vmem = pl.BlockSpec(memory_space=pltpu.VMEM)
    return pl.pallas_call(
        rates_kernel,
        out_shape=(
            jax.ShapeDtypeStruct((4, BLK_DEV * PB), jnp.float32),
            jax.ShapeDtypeStruct((7, BLK_DEV * PB), jnp.float32),
        ),
        in_specs=[smem, smem, vmem, vmem],
        out_specs=(vmem, vmem),
        scratch_shapes=[
            pltpu.VMEM((BLK_DEV + 1, 8, PB), jnp.float32),
            pltpu.VMEM((BLK_DEV + 1, PB, 64), jnp.bfloat16),
            pltpu.VMEM((BLK_DEV + 1, PB, PB), jnp.float32),
            pltpu.VMEM((BLK_DEV + 1, PB, PB), jnp.float32),
            pltpu.VMEM((BLK_DEV + 1, 2, 8, PB), jnp.float32),
            pltpu.VMEM((8, PB), jnp.int32),
            pltpu.VMEM((TOGETHER, 64, 2 * PB), jnp.bfloat16),
            pltpu.VMEM((TOGETHER, PB, 2 * PB), jnp.float32),
            pltpu.VMEM((TOGETHER, 2 * PB, 2 * PB), jnp.bfloat16),
            pltpu.VMEM((TOGETHER, 16, 2 * PB), jnp.bfloat16),
            pltpu.SMEM((8, PB), jnp.int32),
            pltpu.SemaphoreType.DMA,
        ],
        compiler_params=pltpu.CompilerParams(vmem_limit_bytes=16 * 2**20),
        name="tile_rates",
    )(step_index, time_step, lists, gathered)


def on_device(particles, halo_up, halo_down, tile_first, tile_second, tile_live, step_index, time_step):
    mine = jnp.transpose(particles.reshape(8, BLK_DEV, PB), (1, 0, 2))
    gathered, lists = gather(halo_up, halo_down, tile_first, tile_second, tile_live, mine)
    return rates_of(step_index, time_step, lists, gathered.reshape(N_TILE * CHUNK, 8, PB))


def solution(mesh):
    placed = (
        P(None, ("slab", "tile")),
        P(("slab", "tile")),
        P(("slab", "tile")),
        P("slab", "tile"),
        P("slab", "tile"),
        P("slab", "tile"),
        P(),
        P(),
    )
    return jax.shard_map(
        on_device,
        mesh=mesh,
        in_specs=placed,
        out_specs=(P(None, ("slab", "tile")), P(None, ("slab", "tile"))),
        check_vma=False,
    )
```

```python
import heapq
import itertools

import jax
import jax.numpy as jnp
from jax import lax
from jax.experimental import pallas as pl
from jax.experimental.pallas import tpu as pltpu
from jax.sharding import PartitionSpec as P

PB = 128
BLK_DEV = 16
N_SLAB = 16
X, Z = 4, 8
N_TILE = X * Z
CHUNK = 1 + BLK_DEV + 2
NO_TILE = BLK_DEV * 1024

SMOOTHING = 1.0
KERNEL_NORM = 21.0 / (16.0 * 3.141592653589793)
SOUND_SPEED = 10.0
STIFFNESS = SOUND_SPEED * SOUND_SPEED / 7.0
VISCOSITY = 0.1
BLAST_STRENGTH = 8.0
DECAY_TIME = 8.0

MESH = pl.DeviceIdType.MESH

PARTS = (
    dict(first="x", x2="+", z4="+", lo=7, hi=11, at=0.0),
    dict(first="z", x2="-", z4="-", lo=11, hi=16, at=0.1),
    dict(first="z", x2="+", z4="+", lo=0, hi=7, at=0.4),
    dict(first="x", x2="-", z4="-", lo=16, hi=19, at=1.9),
)
BLOCK_US = 4096 / 46.5e3
HOP_US = 2.0


def tree(part):
    x_from = {1: (0, "x+"), 3: (0, "x-"), 2: (1, "x+") if part["x2"] == "+" else (3, "x-")}
    z_from = {1: (0, "z+"), 2: (1, "z+"), 3: (2, "z+"), 7: (0, "z-"), 6: (7, "z-"), 5: (6, "z-")}
    z_from[4] = (3, "z+") if part["z4"] == "+" else (5, "z-")
    children = {}
    for dx, dz in itertools.product(range(X), range(Z)):
        if (dx, dz) == (0, 0):
            continue
        along_z = dz != 0 if part["first"] == "x" else dx == 0
        if along_z:
            parent, way = (dx, z_from[dz][0]), z_from[dz][1]
        else:
            parent, way = (x_from[dx][0], dz), x_from[dx][1]
        children.setdefault(parent, []).append((way, (dx, dz)))
    return children


def schedule():
    trees = [tree(part) for part in PARTS]

    def depth(index, node):
        return max([0] + [1 + depth(index, child) for _, child in trees[index].get(node, [])])

    free = {"x+": 0.0, "x-": 0.0, "z+": 0.0, "z-": 0.0}
    ticket = itertools.count()
    events = [(part["at"], next(ticket), index, (0, 0)) for index, part in enumerate(PARTS)]
    heapq.heapify(events)
    steps = []
    while events:
        now, _, index, node = heapq.heappop(events)
        sends = sorted(trees[index].get(node, []), key=lambda item: -depth(index, item[1]))
        steps.append((index, node, sends))
        blocks = PARTS[index]["hi"] - PARTS[index]["lo"]
        for way, child in sends:
            done = max(now, free[way]) + blocks * BLOCK_US
            free[way] = done
            heapq.heappush(events, (done + HOP_US, next(ticket), index, child))
    return steps


STEPS = schedule()
LEAVES = {(index, node) for index, node, sends in STEPS if not sends}
EARLY = 8


def gather_kernel(up_ref, down_ref, first_ref, second_ref, live_ref, mine_ref,
                  all_ref, codes_ref, centre_ref, left_ref, push_ref, rho_ref,
                  own, rim, slots, fetch_sem, rim_send, rim_recv, send_sem, recv_sem, leaf_sem):
    slab = lax.axis_index("slab")
    tile = lax.axis_index("tile")
    x, z = tile // Z, tile % Z
    above = lax.rem(slab + 1, N_SLAB)
    below = lax.rem(slab + N_SLAB - 1, N_SLAB)
    beside = {
        "x+": lax.rem(x + 1, X) * Z + z,
        "x-": lax.rem(x + X - 1, X) * Z + z,
        "z+": x * Z + lax.rem(z + 1, Z),
        "z-": x * Z + lax.rem(z + Z - 1, Z),
    }
    row = iota((8, PB), 0)

    def held(origin, low, high):
        return all_ref.at[pl.ds(origin * CHUNK + low, high - low)]

    place = pltpu.make_async_copy(mine_ref, held(tile, 1, 1 + BLK_DEV), fetch_sem.at[0])
    load = pltpu.make_async_copy(mine_ref, own, fetch_sem.at[1])
    fetch = [
        pltpu.make_async_copy(ref, slots.at[index], fetch_sem.at[2 + index])
        for index, ref in enumerate((first_ref, second_ref, live_ref))
    ]
    place.start()
    for copy in fetch:
        copy.start()
    load.start()
    barrier = pltpu.get_barrier_semaphore()
    for way in beside:
        pl.semaphore_signal(barrier, inc=1, device_id=(slab, beside[way]), device_id_type=MESH)
    pl.semaphore_signal(barrier, inc=1, device_id=(above, tile), device_id_type=MESH)
    pl.semaphore_signal(barrier, inc=1, device_id=(below, tile), device_id_type=MESH)
    for copy in fetch:
        copy.wait()
    all_ref[tile * CHUNK] = jnp.where(
        row == 0, slots[0], jnp.where(row == 1, slots[1], jnp.where(row == 2, slots[2], 0))
    ).astype(jnp.float32)
    load.wait()
    rim[0] = own[up_ref[0]]
    rim[1] = own[down_ref[0]]
    place.wait()
    pl.semaphore_wait(barrier, 6)

    def rim_copy(side):
        return pltpu.make_async_remote_copy(
            src_ref=rim.at[pl.ds(side, 1)],
            dst_ref=held(tile, 1 + BLK_DEV + side, 2 + BLK_DEV + side),
            send_sem=rim_send.at[side],
            recv_sem=rim_recv.at[side],
            device_id=(above if side == 0 else below, tile),
            device_id_type=MESH,
        )

    def pass_on(where, signal, way):
        return pltpu.make_async_remote_copy(
            src_ref=where,
            dst_ref=where,
            send_sem=send_sem,
            recv_sem=signal,
            device_id=(slab, beside[way]),
            device_id_type=MESH,
        )

    def piece(index, node):
        origin = lax.rem(x + X - node[0], X) * Z + lax.rem(z + Z - node[1], Z)
        return held(origin, PARTS[index]["lo"], PARTS[index]["hi"])

    def arrival(index, node):
        if (index, node) in LEAVES:
            return leaf_sem.at[0 if PARTS[index]["lo"] == 0 else 1]
        return recv_sem.at[index * N_TILE + node[0] * Z + node[1]]

    def one_pair(pair, carry):
        for block in (2 * pair, 2 * pair + 1):
            middle, side = receiver(own[block], row)
            centre_ref[block] = middle
            left_ref[block] = side.astype(jnp.bfloat16)
            push_ref[block] = jnp.broadcast_to(side[:, 56:57], (PB, PB))
            rho_ref[block] = jnp.broadcast_to(side[:, 57:58], (PB, PB))
        return carry

    rims = [rim_copy(0), rim_copy(1)]
    for copy in rims:
        copy.start()
    started = 0
    for index, node, sends in STEPS:
        if (index, node) in LEAVES:
            continue
        where = piece(index, node)
        if node != (0, 0):
            pass_on(where, arrival(index, node), "x+").wait_recv()
        elif PARTS[index]["hi"] == CHUNK:
            lax.fori_loop(0, EARLY // 2, one_pair, 0)
            for copy in rims:
                copy.wait_recv()
        for way, child in sends:
            pass_on(where, arrival(index, child), way).start()
    lax.fori_loop(EARLY // 2, BLK_DEV // 2, one_pair, 0)
    centre_ref[BLK_DEV] = jnp.zeros((8, PB), jnp.float32)
    left_ref[BLK_DEV] = jnp.zeros((PB, 64), jnp.bfloat16)
    push_ref[BLK_DEV] = jnp.zeros((PB, PB), jnp.float32)
    rho_ref[BLK_DEV] = jnp.full((PB, PB), -1.0, jnp.float32)
    listed, other = (sum(PARTS[index]["hi"] - PARTS[index]["lo"] for index, _ in LEAVES
                         if (PARTS[index]["lo"] == 0) == first) for first in (True, False))
    pass_on(all_ref.at[pl.ds(0, listed)], leaf_sem.at[0], "x+").wait_recv()
    codes_ref[...] = choose_tiles(all_ref, slab, tile)
    pass_on(all_ref.at[pl.ds(0, other)], leaf_sem.at[1], "x+").wait_recv()
    for copy in rims:
        copy.wait_send()
    pass_on(all_ref.at[pl.ds(0, (N_TILE - 1) * CHUNK)], leaf_sem.at[0], "x+").wait_send()


def gather(halo_up, halo_down, tile_first, tile_second, tile_live, mine):
    smem = pl.BlockSpec(memory_space=pltpu.SMEM)
    hbm = pl.BlockSpec(memory_space=pltpu.HBM)
    vmem = pl.BlockSpec(memory_space=pltpu.VMEM)
    in_hbm = [
        pltpu.with_memory_space_constraint(array, pltpu.HBM)
        for array in (tile_first, tile_second, tile_live, mine)
    ]
    return pl.pallas_call(
        gather_kernel,
        out_shape=(
            jax.ShapeDtypeStruct((N_TILE * CHUNK, 8, PB), jnp.float32),
            jax.ShapeDtypeStruct((8, PB), jnp.int32),
            jax.ShapeDtypeStruct((BLK_DEV + 1, 8, PB), jnp.float32),
            jax.ShapeDtypeStruct((BLK_DEV + 1, PB, 64), jnp.bfloat16),
            jax.ShapeDtypeStruct((BLK_DEV + 1, PB, PB), jnp.float32),
            jax.ShapeDtypeStruct((BLK_DEV + 1, PB, PB), jnp.float32),
        ),
        in_specs=[smem, smem, hbm, hbm, hbm, hbm],
        out_specs=(vmem,) * 6,
        scratch_shapes=[
            pltpu.VMEM((BLK_DEV, 8, PB), jnp.float32),
            pltpu.VMEM((2, 8, PB), jnp.float32),
            pltpu.VMEM((3, 1, PB), jnp.int32),
            pltpu.SemaphoreType.DMA((5,)),
            pltpu.SemaphoreType.DMA((2,)),
            pltpu.SemaphoreType.DMA((2,)),
            pltpu.SemaphoreType.DMA,
            pltpu.SemaphoreType.DMA((len(PARTS) * N_TILE,)),
            pltpu.SemaphoreType.DMA((2,)),
        ],
        compiler_params=pltpu.CompilerParams(collective_id=0, has_side_effects=True, vmem_limit_bytes=16 * 2**20),
        name="gather_blocks",
    )(halo_up, halo_down, *in_hbm)


def iota(shape, axis):
    return lax.broadcasted_iota(jnp.int32, shape, axis)


def choose_tiles(all_ref, slab, tile):
    first, second, live = (
        jnp.concatenate(
            [all_ref[origin * CHUNK, pl.ds(place, 1)] for origin in range(N_TILE)], axis=0
        ).astype(jnp.int32)
        for place in range(3)
    )
    missing = ((slab == 0) & (second >= 512) & (second < 544)) | ((slab == N_SLAB - 1) & (second >= 544))
    wanted = ((first >> 4) == tile) & (live == 1) & jnp.logical_not(missing)
    source = jnp.where(
        second < 512,
        (second >> 4) * CHUNK + 1 + (second & 15),
        ((second - 512) & 31) * CHUNK + 1 + BLK_DEV + ((second - 512) >> 5),
    )
    code = ((first & 15) * 1024 + source).astype(jnp.float32)
    ones = jnp.where(wanted, 1.0, 0.0)
    upto = (iota((PB, PB), 0) <= iota((PB, PB), 1)).astype(jnp.float32)
    within = jnp.dot(ones, upto, preferred_element_type=jnp.float32)
    earlier = (iota((N_TILE, N_TILE), 1) < iota((N_TILE, N_TILE), 0)).astype(jnp.float32)
    before = jnp.dot(earlier, within, preferred_element_type=jnp.float32)[:, PB - 1 :]
    place = jnp.where(wanted, (before + within).astype(jnp.int32) - 1, -1)
    target = iota((PB, PB), 0)
    chosen = jnp.zeros((PB, PB), jnp.float32)
    for row in range(N_TILE):
        chosen = chosen + jnp.where(place[row : row + 1, :] == target, code[row : row + 1, :], 0.0)
    codes = lax.dot_general(
        jnp.ones((8, PB), jnp.float32), chosen, (((1,), (1,)), ((), ())),
        precision=lax.Precision.HIGHEST, preferred_element_type=jnp.float32,
    )
    count = jnp.sum(before[N_TILE - 1 :, :] + within[N_TILE - 1 :, PB - 1 :])
    row = iota((8, PB), 0)
    codes = jnp.where((row == 0) & (iota((8, PB), 1).astype(jnp.float32) < count), codes, float(NO_TILE))
    return jnp.where(row == 2, count, codes).astype(jnp.int32)


def shifted(rows, up):
    return pltpu.roll(rows, (8 - up) % 8, 0)


def parts_of(value):
    high = value.astype(jnp.bfloat16).astype(jnp.float32)
    rest = value - high
    middle = rest.astype(jnp.bfloat16).astype(jnp.float32)
    return high, middle, rest - middle


def squares_and_products(centred):
    squares = centred * centred
    products = centred * shifted(centred, 3)
    return (
        squares + shifted(squares, 1) + shifted(squares, 2),
        products + shifted(products, 1) + shifted(products, 2),
    )


def pressure_term(density):
    squared = density * density
    return STIFFNESS * (squared * squared * squared * density - 1.0) / squared


def receiver(fields, row):
    centre = jnp.where(row < 6, jnp.broadcast_to(fields[:, 0:1], (8, PB)), 0.0)
    centred = fields - centre
    squares, products = squares_and_products(centred)
    plain = jnp.where(row < 6, centred, jnp.where(row == 6, 1.0, 0.0))
    high, middle, low = parts_of(plain)
    extra = jnp.zeros((8, PB), jnp.float32)
    for place, value in enumerate(parts_of(squares) + parts_of(products)):
        extra = jnp.where(row == place, value if place == 0 else shifted(value, 8 - place), extra)
    pressure = pressure_term(fields)
    columns = jnp.where(row == 0, shifted(pressure, 6), jnp.where(row == 1, shifted(-0.5 * fields, 5), 0.0))
    return centre, jnp.concatenate([high, high, middle, middle, high, low, extra, columns], axis=0).T


def actor_side(centred, row):
    squares, products = squares_and_products(centred)
    for_square = jnp.where(row < 3, -2.0 * centred, jnp.where(row == 6, shifted(squares, 2), 0.0))
    for_approach = jnp.where(
        row < 3, -shifted(centred, 3), jnp.where(row < 6, -shifted(centred, 5), jnp.where(row == 6, shifted(products, 2), 0.0))
    )
    sides = []
    for value, ones in ((for_square, row < 3), (for_approach, (row >= 3) & (row < 6))):
        high, middle, low = parts_of(value)
        extra = jnp.where(ones, 1.0, 0.0)
        sides.append(
            jnp.concatenate([high, middle, high, middle, low, high, extra, jnp.zeros((8, PB), jnp.float32)], axis=0)
        )
    return jnp.concatenate(sides, axis=1).astype(jnp.bfloat16)


TOGETHER = 2


def rates_kernel(step_ref, length_ref, codes, all_ref, centre, left, push, rho, rates_ref, ahead_ref,
                 total, right, squares, factor, moment, plan, plan_sem):
    tile = lax.axis_index("tile")
    row = iota((8, PB), 0)
    copy = pltpu.make_async_copy(codes, plan, plan_sem)
    copy.start()
    total[...] = jnp.zeros_like(total)
    copy.wait()
    number = plan[2, 0]

    def prepare(code, slot):
        right[slot] = actor_side(all_ref[code & 1023] - centre[code >> 10], row)

    def first_product(code, slot):
        squares[slot] = jnp.dot(left[code >> 10], right[slot], preferred_element_type=jnp.float32)

    def elementwise(code, slot):
        a = code >> 10
        fields = all_ref[code & 1023]
        centred = fields - centre[a]
        act_push = jnp.broadcast_to(pressure_term(fields)[6:7], (16, PB))
        act_rho = jnp.broadcast_to(-0.5 * fields[6:7], (16, PB))
        mass = jnp.broadcast_to(fields[7:8] * (5.0 * KERNEL_NORM / 8.0), (8, PB))
        weighted = jnp.where(row == 0, 1.0, shifted(centred, 7)) * mass
        high = weighted.astype(jnp.bfloat16).astype(jnp.float32)
        both = jnp.where(row < 4, high, shifted(weighted - high, 4))
        both = jnp.concatenate([both, jnp.zeros((8, PB), jnp.float32)], axis=0).astype(jnp.bfloat16)
        moment[slot] = jnp.concatenate([both, both], axis=1)
        for low in range(0, PB, 16):
            rows = pl.ds(low, 16)
            dist_sq = jnp.maximum(squares[slot, rows, 0:PB], 1e-30)
            approach = squares[slot, rows, PB : 2 * PB]
            reach = jnp.maximum(2.0 - dist_sq * lax.rsqrt(dist_sq), 0.0)
            weight = reach * reach * reach
            growth = approach * weight
            damping = jnp.minimum(approach, 0.0) / ((dist_sq + 0.01) * (rho[a, rows] + act_rho))
            pressing = (push[a, rows] + act_push + damping) * weight
            for place, value in ((0, pressing), (PB, growth)):
                high = value.astype(jnp.bfloat16)
                factor[slot, pl.ds(place + low, 16), 0:PB] = high
                factor[slot, pl.ds(place + low, 16), PB : 2 * PB] = (value - high.astype(jnp.float32)).astype(jnp.bfloat16)

    def second_product(code, slot):
        a = code >> 10
        sums = lax.dot_general(
            moment[slot], factor[slot], (((1,), (1,)), ((), ())), preferred_element_type=jnp.float32
        )
        total[a, 0] += sums[0:8, 0:PB]
        total[a, 1] += sums[0:8, PB : 2 * PB]

    def one_step(step, stages):
        made, multiplied, weighed = stages
        fresh = [plan[(TOGETHER * step + slot) >> 7, (TOGETHER * step + slot) & 127] for slot in range(TOGETHER)]
        for slot in range(TOGETHER):
            second_product(weighed[slot], slot)
        for slot in range(TOGETHER):
            elementwise(multiplied[slot], slot)
        for slot in range(TOGETHER):
            first_product(made[slot], slot)
        for slot in range(TOGETHER):
            prepare(fresh[slot], slot)
        return fresh, made, multiplied

    nothing = [jnp.int32(NO_TILE)] * TOGETHER
    lax.fori_loop(0, (number + 4 * TOGETHER - 1) // TOGETHER, one_step, (nothing, nothing, nothing))
    length = length_ref[0]
    elapsed = step_ref[0].astype(jnp.float32) * length
    strength = BLAST_STRENGTH * jnp.exp(jnp.full((1, PB), -elapsed / DECAY_TIME, jnp.float32))
    for block in range(BLK_DEV):
        fields = all_ref[tile * CHUNK + 1 + block]
        columns = pl.ds(block * PB, PB)
        moments = total[block, 0, 0:4] + total[block, 0, 4:8]
        growth = -(total[block, 1, 0:1] + total[block, 1, 4:5])
        relative = fields[0:3] + 1.0
        spread_sq = jnp.sum(relative * relative, axis=0, keepdims=True) + 1.0
        source = strength * relative / (spread_sq * jnp.sqrt(spread_sq))
        pushed = (fields - centre[block])[0:3] * moments[0:1] - moments[1:4]
        forcing = pushed + source
        velocity = fields[3:6] + length * forcing
        position = fields[0:3] + length * velocity
        density = fields[6:7] + length * growth
        rates_ref[:, columns] = jnp.concatenate([growth, forcing], axis=0)
        ahead_ref[:, columns] = jnp.concatenate([position, velocity, density], axis=0)


def rates_of(step_index, time_step, gathered):
    smem = pl.BlockSpec(memory_space=pltpu.SMEM)
    vmem = pl.BlockSpec(memory_space=pltpu.VMEM)
    all_blocks, codes, centre, left, push, rho = gathered
    return pl.pallas_call(
        rates_kernel,
        out_shape=(
            jax.ShapeDtypeStruct((4, BLK_DEV * PB), jnp.float32),
            jax.ShapeDtypeStruct((7, BLK_DEV * PB), jnp.float32),
        ),
        in_specs=[smem, smem] + [vmem] * 6,
        out_specs=(vmem, vmem),
        scratch_shapes=[
            pltpu.VMEM((BLK_DEV + 1, 2, 8, PB), jnp.float32),
            pltpu.VMEM((TOGETHER, 64, 2 * PB), jnp.bfloat16),
            pltpu.VMEM((TOGETHER, PB, 2 * PB), jnp.float32),
            pltpu.VMEM((TOGETHER, 2 * PB, 2 * PB), jnp.bfloat16),
            pltpu.VMEM((TOGETHER, 16, 2 * PB), jnp.bfloat16),
            pltpu.SMEM((8, PB), jnp.int32),
            pltpu.SemaphoreType.DMA,
        ],
        compiler_params=pltpu.CompilerParams(vmem_limit_bytes=16 * 2**20),
        name="tile_rates",
    )(step_index, time_step, codes, all_blocks, centre, left, push, rho)


def on_device(particles, halo_up, halo_down, tile_first, tile_second, tile_live, step_index, time_step):
    mine = jnp.transpose(particles.reshape(8, BLK_DEV, PB), (1, 0, 2))
    gathered = gather(halo_up, halo_down, tile_first, tile_second, tile_live, mine)
    return rates_of(step_index, time_step, gathered)


def solution(mesh):
    placed = (
        P(None, ("slab", "tile")),
        P(("slab", "tile")),
        P(("slab", "tile")),
        P("slab", "tile"),
        P("slab", "tile"),
        P("slab", "tile"),
        P(),
        P(),
    )
    return jax.shard_map(
        on_device,
        mesh=mesh,
        in_specs=placed,
        out_specs=(P(None, ("slab", "tile")), P(None, ("slab", "tile"))),
        check_vma=False,
    )
```

```python
import heapq
import itertools

import jax
import jax.numpy as jnp
from jax import lax
from jax.experimental import pallas as pl
from jax.experimental.pallas import tpu as pltpu
from jax.sharding import PartitionSpec as P

PB = 128
BLK_DEV = 16
N_SLAB = 16
X, Z = 4, 8
N_TILE = X * Z
CHUNK = 1 + BLK_DEV + 2
NO_TILE = BLK_DEV * 1024

SMOOTHING = 1.0
KERNEL_NORM = 21.0 / (16.0 * 3.141592653589793)
SOUND_SPEED = 10.0
STIFFNESS = SOUND_SPEED * SOUND_SPEED / 7.0
VISCOSITY = 0.1
BLAST_STRENGTH = 8.0
DECAY_TIME = 8.0

MESH = pl.DeviceIdType.MESH

PARTS = (
    dict(first="x", x2="+", z4="+", lo=7, hi=11, at=0.0),
    dict(first="z", x2="-", z4="-", lo=11, hi=16, at=0.1),
    dict(first="z", x2="+", z4="+", lo=0, hi=7, at=0.4),
    dict(first="x", x2="-", z4="-", lo=16, hi=19, at=1.9),
)
BLOCK_US = 4096 / 46.5e3
HOP_US = 2.0


def tree(part):
    x_from = {1: (0, "x+"), 3: (0, "x-"), 2: (1, "x+") if part["x2"] == "+" else (3, "x-")}
    z_from = {1: (0, "z+"), 2: (1, "z+"), 3: (2, "z+"), 7: (0, "z-"), 6: (7, "z-"), 5: (6, "z-")}
    z_from[4] = (3, "z+") if part["z4"] == "+" else (5, "z-")
    children = {}
    for dx, dz in itertools.product(range(X), range(Z)):
        if (dx, dz) == (0, 0):
            continue
        along_z = dz != 0 if part["first"] == "x" else dx == 0
        if along_z:
            parent, way = (dx, z_from[dz][0]), z_from[dz][1]
        else:
            parent, way = (x_from[dx][0], dz), x_from[dx][1]
        children.setdefault(parent, []).append((way, (dx, dz)))
    return children


def schedule():
    trees = [tree(part) for part in PARTS]

    def depth(index, node):
        return max([0] + [1 + depth(index, child) for _, child in trees[index].get(node, [])])

    free = {"x+": 0.0, "x-": 0.0, "z+": 0.0, "z-": 0.0}
    ticket = itertools.count()
    events = [(part["at"], next(ticket), index, (0, 0)) for index, part in enumerate(PARTS)]
    heapq.heapify(events)
    steps = []
    while events:
        now, _, index, node = heapq.heappop(events)
        sends = sorted(trees[index].get(node, []), key=lambda item: -depth(index, item[1]))
        steps.append((index, node, sends))
        blocks = PARTS[index]["hi"] - PARTS[index]["lo"]
        for way, child in sends:
            done = max(now, free[way]) + blocks * BLOCK_US
            free[way] = done
            heapq.heappush(events, (done + HOP_US, next(ticket), index, child))
    return steps


STEPS = schedule()
LEAVES = {(index, node) for index, node, sends in STEPS if not sends}
EARLY = 8


def gather_kernel(up_ref, down_ref, first_ref, second_ref, live_ref, mine_ref,
                  all_ref, codes_ref, centre_ref, left_ref, push_ref, rho_ref,
                  own, rim, slots, fetch_sem, rim_send, rim_recv, send_sem, recv_sem, leaf_sem):
    slab = lax.axis_index("slab")
    tile = lax.axis_index("tile")
    x, z = tile // Z, tile % Z
    above = lax.rem(slab + 1, N_SLAB)
    below = lax.rem(slab + N_SLAB - 1, N_SLAB)
    beside = {
        "x+": lax.rem(x + 1, X) * Z + z,
        "x-": lax.rem(x + X - 1, X) * Z + z,
        "z+": x * Z + lax.rem(z + 1, Z),
        "z-": x * Z + lax.rem(z + Z - 1, Z),
    }
    row = iota((8, PB), 0)

    def held(origin, low, high):
        return all_ref.at[pl.ds(origin * CHUNK + low, high - low)]

    place = pltpu.make_async_copy(mine_ref, held(tile, 1, 1 + BLK_DEV), fetch_sem.at[0])
    load = pltpu.make_async_copy(mine_ref, own, fetch_sem.at[1])
    fetch = [
        pltpu.make_async_copy(ref, slots.at[index], fetch_sem.at[2 + index])
        for index, ref in enumerate((first_ref, second_ref, live_ref))
    ]
    place.start()
    for copy in fetch:
        copy.start()
    load.start()
    barrier = pltpu.get_barrier_semaphore()
    for way in beside:
        pl.semaphore_signal(barrier, inc=1, device_id=(slab, beside[way]), device_id_type=MESH)
    pl.semaphore_signal(barrier, inc=1, device_id=(above, tile), device_id_type=MESH)
    pl.semaphore_signal(barrier, inc=1, device_id=(below, tile), device_id_type=MESH)
    for copy in fetch:
        copy.wait()
    all_ref[tile * CHUNK] = jnp.where(
        row == 0, slots[0], jnp.where(row == 1, slots[1], jnp.where(row == 2, slots[2], 0))
    ).astype(jnp.float32)
    load.wait()
    rim[0] = own[up_ref[0]]
    rim[1] = own[down_ref[0]]
    place.wait()
    pl.semaphore_wait(barrier, 6)

    def rim_copy(side):
        return pltpu.make_async_remote_copy(
            src_ref=rim.at[pl.ds(side, 1)],
            dst_ref=held(tile, 1 + BLK_DEV + side, 2 + BLK_DEV + side),
            send_sem=rim_send.at[side],
            recv_sem=rim_recv.at[side],
            device_id=(above if side == 0 else below, tile),
            device_id_type=MESH,
        )

    def pass_on(where, signal, way):
        return pltpu.make_async_remote_copy(
            src_ref=where,
            dst_ref=where,
            send_sem=send_sem,
            recv_sem=signal,
            device_id=(slab, beside[way]),
            device_id_type=MESH,
        )

    def piece(index, node):
        origin = lax.rem(x + X - node[0], X) * Z + lax.rem(z + Z - node[1], Z)
        return held(origin, PARTS[index]["lo"], PARTS[index]["hi"])

    def arrival(index, node):
        if (index, node) in LEAVES:
            return leaf_sem.at[0 if PARTS[index]["lo"] == 0 else 1]
        return recv_sem.at[index * N_TILE + node[0] * Z + node[1]]

    def one_pair(pair, carry):
        for block in (2 * pair, 2 * pair + 1):
            middle, side = receiver(own[block], row)
            centre_ref[block] = middle
            left_ref[block] = side.astype(jnp.bfloat16)
            push_ref[block] = jnp.broadcast_to(side[:, 56:57], (PB, PB))
            rho_ref[block] = jnp.broadcast_to(side[:, 57:58], (PB, PB))
        return carry

    rims = [rim_copy(0), rim_copy(1)]
    for copy in rims:
        copy.start()
    started = 0
    for index, node, sends in STEPS:
        if (index, node) in LEAVES:
            continue
        where = piece(index, node)
        if node != (0, 0):
            pass_on(where, arrival(index, node), "x+").wait_recv()
        elif PARTS[index]["hi"] == CHUNK:
            lax.fori_loop(0, EARLY // 2, one_pair, 0)
            for copy in rims:
                copy.wait_recv()
        for way, child in sends:
            pass_on(where, arrival(index, child), way).start()
    lax.fori_loop(EARLY // 2, BLK_DEV // 2, one_pair, 0)
    centre_ref[BLK_DEV] = jnp.zeros((8, PB), jnp.float32)
    left_ref[BLK_DEV] = jnp.zeros((PB, 64), jnp.bfloat16)
    push_ref[BLK_DEV] = jnp.zeros((PB, PB), jnp.float32)
    rho_ref[BLK_DEV] = jnp.full((PB, PB), -1.0, jnp.float32)
    listed, other = (sum(PARTS[index]["hi"] - PARTS[index]["lo"] for index, _ in LEAVES
                         if (PARTS[index]["lo"] == 0) == first) for first in (True, False))
    pass_on(all_ref.at[pl.ds(0, listed)], leaf_sem.at[0], "x+").wait_recv()
    codes_ref[...] = choose_tiles(all_ref, slab, tile)
    pass_on(all_ref.at[pl.ds(0, other)], leaf_sem.at[1], "x+").wait_recv()
    for copy in rims:
        copy.wait_send()
    pass_on(all_ref.at[pl.ds(0, (N_TILE - 1) * CHUNK)], leaf_sem.at[0], "x+").wait_send()


def gather(halo_up, halo_down, tile_first, tile_second, tile_live, mine):
    smem = pl.BlockSpec(memory_space=pltpu.SMEM)
    hbm = pl.BlockSpec(memory_space=pltpu.HBM)
    vmem = pl.BlockSpec(memory_space=pltpu.VMEM)
    in_hbm = [
        pltpu.with_memory_space_constraint(array, pltpu.HBM)
        for array in (tile_first, tile_second, tile_live, mine)
    ]
    return pl.pallas_call(
        gather_kernel,
        out_shape=(
            jax.ShapeDtypeStruct((N_TILE * CHUNK, 8, PB), jnp.float32),
            jax.ShapeDtypeStruct((8, PB), jnp.int32),
            jax.ShapeDtypeStruct((BLK_DEV + 1, 8, PB), jnp.float32),
            jax.ShapeDtypeStruct((BLK_DEV + 1, PB, 64), jnp.bfloat16),
            jax.ShapeDtypeStruct((BLK_DEV + 1, PB, PB), jnp.float32),
            jax.ShapeDtypeStruct((BLK_DEV + 1, PB, PB), jnp.float32),
        ),
        in_specs=[smem, smem, hbm, hbm, hbm, hbm],
        out_specs=(vmem,) * 6,
        scratch_shapes=[
            pltpu.VMEM((BLK_DEV, 8, PB), jnp.float32),
            pltpu.VMEM((2, 8, PB), jnp.float32),
            pltpu.VMEM((3, 1, PB), jnp.int32),
            pltpu.SemaphoreType.DMA((5,)),
            pltpu.SemaphoreType.DMA((2,)),
            pltpu.SemaphoreType.DMA((2,)),
            pltpu.SemaphoreType.DMA,
            pltpu.SemaphoreType.DMA((len(PARTS) * N_TILE,)),
            pltpu.SemaphoreType.DMA((2,)),
        ],
        compiler_params=pltpu.CompilerParams(collective_id=0, has_side_effects=True, vmem_limit_bytes=16 * 2**20),
        name="gather_blocks",
    )(halo_up, halo_down, *in_hbm)


def iota(shape, axis):
    return lax.broadcasted_iota(jnp.int32, shape, axis)


def choose_tiles(all_ref, slab, tile):
    first, second, live = (
        jnp.concatenate(
            [all_ref[origin * CHUNK, pl.ds(place, 1)] for origin in range(N_TILE)], axis=0
        ).astype(jnp.int32)
        for place in range(3)
    )
    missing = ((slab == 0) & (second >= 512) & (second < 544)) | ((slab == N_SLAB - 1) & (second >= 544))
    wanted = ((first >> 4) == tile) & (live == 1) & jnp.logical_not(missing)
    source = jnp.where(
        second < 512,
        (second >> 4) * CHUNK + 1 + (second & 15),
        ((second - 512) & 31) * CHUNK + 1 + BLK_DEV + ((second - 512) >> 5),
    )
    code = ((first & 15) * 1024 + source).astype(jnp.float32)
    ones = jnp.where(wanted, 1.0, 0.0)
    upto = (iota((PB, PB), 0) <= iota((PB, PB), 1)).astype(jnp.float32)
    within = jnp.dot(ones, upto, preferred_element_type=jnp.float32)
    earlier = (iota((N_TILE, N_TILE), 1) < iota((N_TILE, N_TILE), 0)).astype(jnp.float32)
    before = jnp.dot(earlier, within, preferred_element_type=jnp.float32)[:, PB - 1 :]
    place = jnp.where(wanted, (before + within).astype(jnp.int32) - 1, -1)
    target = iota((PB, PB), 0)
    chosen = jnp.zeros((PB, PB), jnp.float32)
    for row in range(N_TILE):
        chosen = chosen + jnp.where(place[row : row + 1, :] == target, code[row : row + 1, :], 0.0)
    codes = lax.dot_general(
        jnp.ones((8, PB), jnp.float32), chosen, (((1,), (1,)), ((), ())),
        precision=lax.Precision.HIGHEST, preferred_element_type=jnp.float32,
    )
    count = jnp.sum(before[N_TILE - 1 :, :] + within[N_TILE - 1 :, PB - 1 :])
    row = iota((8, PB), 0)
    codes = jnp.where((row == 0) & (iota((8, PB), 1).astype(jnp.float32) < count), codes, float(NO_TILE))
    return jnp.where(row == 2, count, codes).astype(jnp.int32)


def shifted(rows, up):
    return pltpu.roll(rows, (8 - up) % 8, 0)


def parts_of(value):
    high = value.astype(jnp.bfloat16).astype(jnp.float32)
    rest = value - high
    middle = rest.astype(jnp.bfloat16).astype(jnp.float32)
    return high, middle, rest - middle


def squares_and_products(centred):
    squares = centred * centred
    products = centred * shifted(centred, 3)
    return (
        squares + shifted(squares, 1) + shifted(squares, 2),
        products + shifted(products, 1) + shifted(products, 2),
    )


def pressure_term(density):
    squared = density * density
    return STIFFNESS * (squared * squared * squared * density - 1.0) / squared


def receiver(fields, row):
    centre = jnp.where(row < 6, jnp.broadcast_to(fields[:, 0:1], (8, PB)), 0.0)
    centred = fields - centre
    squares, products = squares_and_products(centred)
    plain = jnp.where(row < 6, centred, jnp.where(row == 6, 1.0, 0.0))
    high, middle, low = parts_of(plain)
    extra = jnp.zeros((8, PB), jnp.float32)
    for place, value in enumerate(parts_of(squares) + parts_of(products)):
        extra = jnp.where(row == place, value if place == 0 else shifted(value, 8 - place), extra)
    pressure = pressure_term(fields)
    columns = jnp.where(row == 0, shifted(pressure, 6), jnp.where(row == 1, shifted(-0.5 * fields, 5), 0.0))
    return centre, jnp.concatenate([high, high, middle, middle, high, low, extra, columns], axis=0).T


def actor_side(centred, row):
    squares, products = squares_and_products(centred)
    for_square = jnp.where(row < 3, -2.0 * centred, jnp.where(row == 6, shifted(squares, 2), 0.0))
    for_approach = jnp.where(
        row < 3, -shifted(centred, 3), jnp.where(row < 6, -shifted(centred, 5), jnp.where(row == 6, shifted(products, 2), 0.0))
    )
    sides = []
    for value, ones in ((for_square, row < 3), (for_approach, (row >= 3) & (row < 6))):
        high, middle, low = parts_of(value)
        extra = jnp.where(ones, 1.0, 0.0)
        sides.append(
            jnp.concatenate([high, middle, high, middle, low, high, extra, jnp.zeros((8, PB), jnp.float32)], axis=0)
        )
    return jnp.concatenate(sides, axis=1).astype(jnp.bfloat16)


TOGETHER = 3


def rates_kernel(step_ref, length_ref, codes, all_ref, centre, left, push, rho, rates_ref, ahead_ref,
                 total, right, squares, factor, moment, acts, plan, plan_sem):
    tile = lax.axis_index("tile")
    row = iota((8, PB), 0)
    copy = pltpu.make_async_copy(codes, plan, plan_sem)
    copy.start()
    total[...] = jnp.zeros_like(total)
    copy.wait()
    number = plan[2, 0]

    def prepare(code, slot):
        fields = all_ref[code & 1023]
        centred = fields - centre[code >> 10]
        right[slot] = actor_side(centred, row)
        mass = jnp.broadcast_to(fields[7:8] * (5.0 * KERNEL_NORM / 8.0), (8, PB))
        weighted = jnp.where(row == 0, 1.0, shifted(centred, 7)) * mass
        high = weighted.astype(jnp.bfloat16).astype(jnp.float32)
        both = jnp.where(row < 4, high, shifted(weighted - high, 4))
        both = jnp.concatenate([both, jnp.zeros((8, PB), jnp.float32)], axis=0).astype(jnp.bfloat16)
        moment[0, slot] = jnp.concatenate([both, both], axis=1)
        acts[0, slot] = jnp.where(row == 6, pressure_term(fields), -0.5 * shifted(fields, 7))

    def first_product(code, slot):
        squares[slot] = jnp.dot(left[code >> 10], right[slot], preferred_element_type=jnp.float32)
        moment[1, slot] = moment[0, slot]
        acts[1, slot] = acts[0, slot]

    def elementwise(code, slot):
        a = code >> 10
        act_push = jnp.broadcast_to(acts[1, slot, 6:7], (16, PB))
        act_rho = jnp.broadcast_to(acts[1, slot, 7:8], (16, PB))
        for low in range(0, PB, 16):
            rows = pl.ds(low, 16)
            dist_sq = jnp.maximum(squares[slot, rows, 0:PB], 1e-30)
            approach = squares[slot, rows, PB : 2 * PB]
            reach = jnp.maximum(2.0 - dist_sq * lax.rsqrt(dist_sq), 0.0)
            weight = reach * reach * reach
            growth = approach * weight
            damping = jnp.minimum(approach, 0.0) / ((dist_sq + 0.01) * (rho[a, rows] + act_rho))
            pressing = (push[a, rows] + act_push + damping) * weight
            for place, value in ((0, pressing), (PB, growth)):
                high = value.astype(jnp.bfloat16)
                lower = (value - high.astype(jnp.float32)).astype(jnp.bfloat16)
                factor[slot, pl.ds(place + low, 16), 0:PB] = high
                factor[slot, pl.ds(place + low, 16), PB : 2 * PB] = lower
        moment[2, slot] = moment[1, slot]

    def second_product(code, slot):
        a = code >> 10
        sums = lax.dot_general(
            moment[2, slot], factor[slot], (((1,), (1,)), ((), ())), preferred_element_type=jnp.float32
        )
        total[a, 0] += sums[0:8, 0:PB]
        total[a, 1] += sums[0:8, PB : 2 * PB]

    def one_step(step, stages):
        fresh = [plan[(TOGETHER * step + slot) >> 7, (TOGETHER * step + slot) & 127] for slot in range(TOGETHER)]
        made, multiplied, weighed = stages
        for slot in range(TOGETHER):
            second_product(weighed[slot], slot)
        for slot in range(TOGETHER):
            elementwise(multiplied[slot], slot)
        for slot in range(TOGETHER):
            first_product(made[slot], slot)
        for slot in range(TOGETHER):
            prepare(fresh[slot], slot)
        return fresh, made, multiplied

    nothing = [jnp.int32(NO_TILE)] * TOGETHER
    lax.fori_loop(0, (number + 4 * TOGETHER - 1) // TOGETHER, one_step, (nothing, nothing, nothing))
    length = length_ref[0]
    elapsed = step_ref[0].astype(jnp.float32) * length
    strength = BLAST_STRENGTH * jnp.exp(jnp.full((1, PB), -elapsed / DECAY_TIME, jnp.float32))
    for block in range(BLK_DEV):
        fields = all_ref[tile * CHUNK + 1 + block]
        columns = pl.ds(block * PB, PB)
        moments = total[block, 0, 0:4] + total[block, 0, 4:8]
        growth = -(total[block, 1, 0:1] + total[block, 1, 4:5])
        relative = fields[0:3] + 1.0
        spread_sq = jnp.sum(relative * relative, axis=0, keepdims=True) + 1.0
        source = strength * relative / (spread_sq * jnp.sqrt(spread_sq))
        pushed = (fields - centre[block])[0:3] * moments[0:1] - moments[1:4]
        forcing = pushed + source
        velocity = fields[3:6] + length * forcing
        position = fields[0:3] + length * velocity
        density = fields[6:7] + length * growth
        rates_ref[:, columns] = jnp.concatenate([growth, forcing], axis=0)
        ahead_ref[:, columns] = jnp.concatenate([position, velocity, density], axis=0)


def rates_of(step_index, time_step, gathered):
    smem = pl.BlockSpec(memory_space=pltpu.SMEM)
    vmem = pl.BlockSpec(memory_space=pltpu.VMEM)
    all_blocks, codes, centre, left, push, rho = gathered
    return pl.pallas_call(
        rates_kernel,
        out_shape=(
            jax.ShapeDtypeStruct((4, BLK_DEV * PB), jnp.float32),
            jax.ShapeDtypeStruct((7, BLK_DEV * PB), jnp.float32),
        ),
        in_specs=[smem, smem] + [vmem] * 6,
        out_specs=(vmem, vmem),
        scratch_shapes=[
            pltpu.VMEM((BLK_DEV + 1, 2, 8, PB), jnp.float32),
            pltpu.VMEM((TOGETHER, 64, 2 * PB), jnp.bfloat16),
            pltpu.VMEM((TOGETHER, PB, 2 * PB), jnp.float32),
            pltpu.VMEM((TOGETHER, 2 * PB, 2 * PB), jnp.bfloat16),
            pltpu.VMEM((3, TOGETHER, 16, 2 * PB), jnp.bfloat16),
            pltpu.VMEM((2, TOGETHER, 8, PB), jnp.float32),
            pltpu.SMEM((8, PB), jnp.int32),
            pltpu.SemaphoreType.DMA,
        ],
        compiler_params=pltpu.CompilerParams(vmem_limit_bytes=16 * 2**20),
        name="tile_rates",
    )(step_index, time_step, codes, all_blocks, centre, left, push, rho)


def on_device(particles, halo_up, halo_down, tile_first, tile_second, tile_live, step_index, time_step):
    mine = jnp.transpose(particles.reshape(8, BLK_DEV, PB), (1, 0, 2))
    gathered = gather(halo_up, halo_down, tile_first, tile_second, tile_live, mine)
    return rates_of(step_index, time_step, gathered)


def solution(mesh):
    placed = (
        P(None, ("slab", "tile")),
        P(("slab", "tile")),
        P(("slab", "tile")),
        P("slab", "tile"),
        P("slab", "tile"),
        P("slab", "tile"),
        P(),
        P(),
    )
    return jax.shard_map(
        on_device,
        mesh=mesh,
        in_specs=placed,
        out_specs=(P(None, ("slab", "tile")), P(None, ("slab", "tile"))),
        check_vma=False,
    )
```

```python
import heapq
import itertools

import jax
import jax.numpy as jnp
from jax import lax
from jax.experimental import pallas as pl
from jax.experimental.pallas import tpu as pltpu
from jax.sharding import PartitionSpec as P

PB = 128
BLK_DEV = 16
N_SLAB = 16
X, Z = 4, 8
N_TILE = X * Z
CHUNK = 1 + BLK_DEV + 2
NO_TILE = BLK_DEV * 1024

SMOOTHING = 1.0
KERNEL_NORM = 21.0 / (16.0 * 3.141592653589793)
SOUND_SPEED = 10.0
STIFFNESS = SOUND_SPEED * SOUND_SPEED / 7.0
VISCOSITY = 0.1
BLAST_STRENGTH = 8.0
DECAY_TIME = 8.0

MESH = pl.DeviceIdType.MESH

PARTS = (
    dict(first="x", x2="+", z4="+", lo=13, hi=19, at=1.9),
    dict(first="z", x2="-", z4="-", lo=7, hi=13, at=0.1),
    dict(first="z", x2="+", z4="+", lo=0, hi=7, at=0.4),
)
BLOCK_US = 4096 / 46.5e3
HOP_US = 3.0


def tree(part):
    x_from = {1: (0, "x+"), 3: (0, "x-"), 2: (1, "x+") if part["x2"] == "+" else (3, "x-")}
    z_from = {1: (0, "z+"), 2: (1, "z+"), 3: (2, "z+"), 7: (0, "z-"), 6: (7, "z-"), 5: (6, "z-")}
    z_from[4] = (3, "z+") if part["z4"] == "+" else (5, "z-")
    children = {}
    for dx, dz in itertools.product(range(X), range(Z)):
        if (dx, dz) == (0, 0):
            continue
        along_z = dz != 0 if part["first"] == "x" else dx == 0
        if along_z:
            parent, way = (dx, z_from[dz][0]), z_from[dz][1]
        else:
            parent, way = (x_from[dx][0], dz), x_from[dx][1]
        children.setdefault(parent, []).append((way, (dx, dz)))
    return children


def schedule():
    trees = [tree(part) for part in PARTS]

    def depth(index, node):
        return max([0] + [1 + depth(index, child) for _, child in trees[index].get(node, [])])

    free = {"x+": 0.0, "x-": 0.0, "z+": 0.0, "z-": 0.0}
    ticket = itertools.count()
    events = [(part["at"], next(ticket), index, (0, 0)) for index, part in enumerate(PARTS)]
    heapq.heapify(events)
    steps = []
    while events:
        now, _, index, node = heapq.heappop(events)
        sends = sorted(trees[index].get(node, []), key=lambda item: -depth(index, item[1]))
        steps.append((index, node, sends))
        blocks = PARTS[index]["hi"] - PARTS[index]["lo"]
        for way, child in sends:
            done = max(now, free[way]) + blocks * BLOCK_US
            free[way] = done
            heapq.heappush(events, (done + HOP_US, next(ticket), index, child))
    return steps


STEPS = schedule()
LEAVES = {(index, node) for index, node, sends in STEPS if not sends}
EARLY = 8


def gather_kernel(up_ref, down_ref, first_ref, second_ref, live_ref, mine_ref,
                  all_ref, codes_ref, centre_ref, left_ref, push_ref, rho_ref,
                  own, rim, slots, fetch_sem, rim_send, rim_recv, send_sem, recv_sem, leaf_sem):
    slab = lax.axis_index("slab")
    tile = lax.axis_index("tile")
    x, z = tile // Z, tile % Z
    above = lax.rem(slab + 1, N_SLAB)
    below = lax.rem(slab + N_SLAB - 1, N_SLAB)
    beside = {
        "x+": lax.rem(x + 1, X) * Z + z,
        "x-": lax.rem(x + X - 1, X) * Z + z,
        "z+": x * Z + lax.rem(z + 1, Z),
        "z-": x * Z + lax.rem(z + Z - 1, Z),
    }
    row = iota((8, PB), 0)

    def held(origin, low, high):
        return all_ref.at[pl.ds(origin * CHUNK + low, high - low)]

    place = pltpu.make_async_copy(mine_ref, held(tile, 1, 1 + BLK_DEV), fetch_sem.at[0])
    load = pltpu.make_async_copy(mine_ref, own, fetch_sem.at[1])
    fetch = [
        pltpu.make_async_copy(ref, slots.at[index], fetch_sem.at[2 + index])
        for index, ref in enumerate((first_ref, second_ref, live_ref))
    ]
    place.start()
    for copy in fetch:
        copy.start()
    load.start()
    barrier = pltpu.get_barrier_semaphore()
    for way in beside:
        pl.semaphore_signal(barrier, inc=1, device_id=(slab, beside[way]), device_id_type=MESH)
    pl.semaphore_signal(barrier, inc=1, device_id=(above, tile), device_id_type=MESH)
    pl.semaphore_signal(barrier, inc=1, device_id=(below, tile), device_id_type=MESH)
    pl.semaphore_wait(barrier, 6)

    def rim_copy(side):
        return pltpu.make_async_remote_copy(
            src_ref=rim.at[pl.ds(side, 1)],
            dst_ref=held(tile, 1 + BLK_DEV + side, 2 + BLK_DEV + side),
            send_sem=rim_send.at[side],
            recv_sem=rim_recv.at[side],
            device_id=(above if side == 0 else below, tile),
            device_id_type=MESH,
        )

    def pass_on(where, signal, way, source=None):
        return pltpu.make_async_remote_copy(
            src_ref=where if source is None else source,
            dst_ref=where,
            send_sem=send_sem,
            recv_sem=signal,
            device_id=(slab, beside[way]),
            device_id_type=MESH,
        )

    def piece(index, node):
        origin = lax.rem(x + X - node[0], X) * Z + lax.rem(z + Z - node[1], Z)
        return held(origin, PARTS[index]["lo"], PARTS[index]["hi"])

    def arrival(index, node):
        if (index, node) in LEAVES:
            return leaf_sem.at[0 if PARTS[index]["lo"] == 0 else 1]
        return recv_sem.at[index * N_TILE + node[0] * Z + node[1]]

    def one_pair(pair, carry):
        for block in (2 * pair, 2 * pair + 1):
            middle, side = receiver(own[block], row)
            centre_ref[block] = middle
            left_ref[block] = side.astype(jnp.bfloat16)
            push_ref[block] = jnp.broadcast_to(side[:, 56:57], (PB, PB))
            rho_ref[block] = jnp.broadcast_to(side[:, 57:58], (PB, PB))
        return carry

    rims = [rim_copy(0), rim_copy(1)]
    for index, node, sends in STEPS:
        part = PARTS[index]
        if node == (0, 0) and part["lo"] > 0 and part["hi"] <= 1 + BLK_DEV:
            for way, child in sends:
                source = mine_ref.at[pl.ds(part["lo"] - 1, part["hi"] - part["lo"])]
                pass_on(piece(index, node), arrival(index, child), way, source).start()
    for copy in fetch:
        copy.wait()
    all_ref[tile * CHUNK] = jnp.where(
        row == 0, slots[0], jnp.where(row == 1, slots[1], jnp.where(row == 2, slots[2], 0))
    ).astype(jnp.float32)
    load.wait()
    rim[0] = own[up_ref[0]]
    rim[1] = own[down_ref[0]]
    lax.fori_loop(0, 1, one_pair, 0)
    for copy in rims:
        copy.start()
    place.wait()
    for index, node, sends in STEPS:
        if (index, node) in LEAVES:
            continue
        part = PARTS[index]
        if node == (0, 0) and part["lo"] > 0 and part["hi"] <= 1 + BLK_DEV:
            continue
        where = piece(index, node)
        if node != (0, 0):
            pass_on(where, arrival(index, node), "x+").wait_recv()
        elif part["hi"] == CHUNK:
            lax.fori_loop(1, EARLY // 2, one_pair, 0)
            for copy in rims:
                copy.wait_recv()
        for way, child in sends:
            pass_on(where, arrival(index, child), way).start()
    lax.fori_loop(EARLY // 2, BLK_DEV // 2, one_pair, 0)
    centre_ref[BLK_DEV] = jnp.zeros((8, PB), jnp.float32)
    left_ref[BLK_DEV] = jnp.zeros((PB, 64), jnp.bfloat16)
    push_ref[BLK_DEV] = jnp.zeros((PB, PB), jnp.float32)
    rho_ref[BLK_DEV] = jnp.full((PB, PB), -1.0, jnp.float32)
    listed, other = (sum(PARTS[index]["hi"] - PARTS[index]["lo"] for index, _ in LEAVES
                         if (PARTS[index]["lo"] == 0) == first) for first in (True, False))
    pass_on(all_ref.at[pl.ds(0, listed)], leaf_sem.at[0], "x+").wait_recv()
    codes_ref[...] = choose_tiles(all_ref, slab, tile)
    pass_on(all_ref.at[pl.ds(0, other)], leaf_sem.at[1], "x+").wait_recv()
    for copy in rims:
        copy.wait_send()
    pass_on(all_ref.at[pl.ds(0, (N_TILE - 1) * CHUNK)], leaf_sem.at[0], "x+").wait_send()


def gather(halo_up, halo_down, tile_first, tile_second, tile_live, mine):
    smem = pl.BlockSpec(memory_space=pltpu.SMEM)
    hbm = pl.BlockSpec(memory_space=pltpu.HBM)
    vmem = pl.BlockSpec(memory_space=pltpu.VMEM)
    in_hbm = [
        pltpu.with_memory_space_constraint(array, pltpu.HBM)
        for array in (tile_first, tile_second, tile_live, mine)
    ]
    return pl.pallas_call(
        gather_kernel,
        out_shape=(
            jax.ShapeDtypeStruct((N_TILE * CHUNK, 8, PB), jnp.float32),
            jax.ShapeDtypeStruct((8, PB), jnp.int32),
            jax.ShapeDtypeStruct((BLK_DEV + 1, 8, PB), jnp.float32),
            jax.ShapeDtypeStruct((BLK_DEV + 1, PB, 64), jnp.bfloat16),
            jax.ShapeDtypeStruct((BLK_DEV + 1, PB, PB), jnp.float32),
            jax.ShapeDtypeStruct((BLK_DEV + 1, PB, PB), jnp.float32),
        ),
        in_specs=[smem, smem, hbm, hbm, hbm, hbm],
        out_specs=(vmem,) * 6,
        scratch_shapes=[
            pltpu.VMEM((BLK_DEV, 8, PB), jnp.float32),
            pltpu.VMEM((2, 8, PB), jnp.float32),
            pltpu.VMEM((3, 1, PB), jnp.int32),
            pltpu.SemaphoreType.DMA((5,)),
            pltpu.SemaphoreType.DMA((2,)),
            pltpu.SemaphoreType.DMA((2,)),
            pltpu.SemaphoreType.DMA,
            pltpu.SemaphoreType.DMA((len(PARTS) * N_TILE,)),
            pltpu.SemaphoreType.DMA((2,)),
        ],
        compiler_params=pltpu.CompilerParams(collective_id=0, has_side_effects=True, vmem_limit_bytes=16 * 2**20),
        name="gather_blocks",
    )(halo_up, halo_down, *in_hbm)


def iota(shape, axis):
    return lax.broadcasted_iota(jnp.int32, shape, axis)


def choose_tiles(all_ref, slab, tile):
    first, second, live = (
        jnp.concatenate(
            [all_ref[origin * CHUNK, pl.ds(place, 1)] for origin in range(N_TILE)], axis=0
        ).astype(jnp.int32)
        for place in range(3)
    )
    missing = ((slab == 0) & (second >= 512) & (second < 544)) | ((slab == N_SLAB - 1) & (second >= 544))
    wanted = ((first >> 4) == tile) & (live == 1) & jnp.logical_not(missing)
    source = jnp.where(
        second < 512,
        (second >> 4) * CHUNK + 1 + (second & 15),
        ((second - 512) & 31) * CHUNK + 1 + BLK_DEV + ((second - 512) >> 5),
    )
    code = ((first & 15) * 1024 + source).astype(jnp.float32)
    ones = jnp.where(wanted, 1.0, 0.0)
    upto = (iota((PB, PB), 0) <= iota((PB, PB), 1)).astype(jnp.float32)
    within = jnp.dot(ones, upto, preferred_element_type=jnp.float32)
    earlier = (iota((N_TILE, N_TILE), 1) < iota((N_TILE, N_TILE), 0)).astype(jnp.float32)
    before = jnp.dot(earlier, within, preferred_element_type=jnp.float32)[:, PB - 1 :]
    place = jnp.where(wanted, (before + within).astype(jnp.int32) - 1, -1)
    target = iota((PB, PB), 0)
    chosen = jnp.zeros((PB, PB), jnp.float32)
    for row in range(N_TILE):
        chosen = chosen + jnp.where(place[row : row + 1, :] == target, code[row : row + 1, :], 0.0)
    codes = lax.dot_general(
        jnp.ones((8, PB), jnp.float32), chosen, (((1,), (1,)), ((), ())),
        precision=lax.Precision.HIGHEST, preferred_element_type=jnp.float32,
    )
    count = jnp.sum(before[N_TILE - 1 :, :] + within[N_TILE - 1 :, PB - 1 :])
    row = iota((8, PB), 0)
    codes = jnp.where((row == 0) & (iota((8, PB), 1).astype(jnp.float32) < count), codes, float(NO_TILE))
    return jnp.where(row == 2, count, codes).astype(jnp.int32)


def shifted(rows, up):
    return pltpu.roll(rows, (8 - up) % 8, 0)


def parts_of(value):
    high = value.astype(jnp.bfloat16).astype(jnp.float32)
    rest = value - high
    middle = rest.astype(jnp.bfloat16).astype(jnp.float32)
    return high, middle, rest - middle


def squares_and_products(centred):
    squares = centred * centred
    products = centred * shifted(centred, 3)
    return (
        squares + shifted(squares, 1) + shifted(squares, 2),
        products + shifted(products, 1) + shifted(products, 2),
    )


def pressure_term(density):
    squared = density * density
    return STIFFNESS * (squared * squared * squared * density - 1.0) / squared


def receiver(fields, row):
    centre = jnp.where(row < 6, jnp.broadcast_to(fields[:, 0:1], (8, PB)), 0.0)
    centred = fields - centre
    squares, products = squares_and_products(centred)
    plain = jnp.where(row < 6, centred, jnp.where(row == 6, 1.0, 0.0))
    high, middle, low = parts_of(plain)
    extra = jnp.zeros((8, PB), jnp.float32)
    for place, value in enumerate(parts_of(squares) + parts_of(products)):
        extra = jnp.where(row == place, value if place == 0 else shifted(value, 8 - place), extra)
    pressure = pressure_term(fields)
    columns = jnp.where(row == 0, shifted(pressure, 6), jnp.where(row == 1, shifted(-0.5 * fields, 5), 0.0))
    return centre, jnp.concatenate([high, high, middle, middle, high, low, extra, columns], axis=0).T


def actor_side(centred, row):
    squares, products = squares_and_products(centred)
    for_square = jnp.where(row < 3, -2.0 * centred, jnp.where(row == 6, shifted(squares, 2), 0.0))
    for_approach = jnp.where(
        row < 3, -shifted(centred, 3), jnp.where(row < 6, -shifted(centred, 5), jnp.where(row == 6, shifted(products, 2), 0.0))
    )
    sides = []
    for value, ones in ((for_square, row < 3), (for_approach, (row >= 3) & (row < 6))):
        high, middle, low = parts_of(value)
        extra = jnp.where(ones, 1.0, 0.0)
        sides.append(
            jnp.concatenate([high, middle, high, middle, low, high, extra, jnp.zeros((8, PB), jnp.float32)], axis=0)
        )
    return jnp.concatenate(sides, axis=1).astype(jnp.bfloat16)


TOGETHER = 3


def rates_kernel(step_ref, length_ref, codes, all_ref, centre, left, push, rho, rates_ref, ahead_ref,
                 total, right, squares, factor, moment, acts, plan, plan_sem):
    tile = lax.axis_index("tile")
    row = iota((8, PB), 0)
    copy = pltpu.make_async_copy(codes, plan, plan_sem)
    copy.start()
    total[...] = jnp.zeros_like(total)
    copy.wait()
    number = plan[2, 0]

    def prepare(code, slot):
        fields = all_ref[code & 1023]
        centred = fields - centre[code >> 10]
        right[slot] = actor_side(centred, row)
        mass = jnp.broadcast_to(fields[7:8] * (5.0 * KERNEL_NORM / 8.0), (8, PB))
        weighted = jnp.where(row == 0, 1.0, shifted(centred, 7)) * mass
        high = weighted.astype(jnp.bfloat16).astype(jnp.float32)
        both = jnp.where(row < 4, high, shifted(weighted - high, 4))
        both = jnp.concatenate([both, jnp.zeros((8, PB), jnp.float32)], axis=0).astype(jnp.bfloat16)
        moment[0, slot] = jnp.concatenate([both, both], axis=1)
        acts[0, slot] = jnp.where(row == 6, pressure_term(fields), -0.5 * shifted(fields, 7))

    def first_product(code, slot):
        squares[slot] = jnp.dot(left[code >> 10], right[slot], preferred_element_type=jnp.float32)
        moment[1, slot] = moment[0, slot]
        acts[1, slot] = acts[0, slot]

    def elementwise(code, slot):
        a = code >> 10
        act_push = jnp.broadcast_to(acts[1, slot, 6:7], (16, PB))
        act_rho = jnp.broadcast_to(acts[1, slot, 7:8], (16, PB))
        for low in range(0, PB, 16):
            rows = pl.ds(low, 16)
            dist_sq = jnp.maximum(squares[slot, rows, 0:PB], 1e-30)
            approach = squares[slot, rows, PB : 2 * PB]
            reach = jnp.maximum(2.0 - dist_sq * lax.rsqrt(dist_sq), 0.0)
            weight = reach * reach * reach
            growth = approach * weight
            damping = jnp.minimum(approach, 0.0) / ((dist_sq + 0.01) * (rho[a, rows] + act_rho))
            pressing = (push[a, rows] + act_push + damping) * weight
            for place, value in ((0, pressing), (PB, growth)):
                high = value.astype(jnp.bfloat16)
                lower = (value - high.astype(jnp.float32)).astype(jnp.bfloat16)
                factor[slot, pl.ds(place + low, 16), 0:PB] = high
                factor[slot, pl.ds(place + low, 16), PB : 2 * PB] = lower
        moment[2, slot] = moment[1, slot]

    def second_product(code, slot):
        a = code >> 10
        sums = lax.dot_general(
            moment[2, slot], factor[slot], (((1,), (1,)), ((), ())), preferred_element_type=jnp.float32
        )
        total[a, 0] += sums[0:8, 0:PB]
        total[a, 1] += sums[0:8, PB : 2 * PB]

    def group(step):
        return [plan[(TOGETHER * step + slot) >> 7, (TOGETHER * step + slot) & 127] for slot in range(TOGETHER)]

    def stage(work, codes_now):
        for slot in range(TOGETHER):
            work(codes_now[slot], slot)

    def one_step(step, stages):
        made, multiplied, weighed = stages
        fresh = group(step)
        stage(second_product, weighed)
        stage(elementwise, multiplied)
        stage(first_product, made)
        stage(prepare, fresh)
        return fresh, made, multiplied

    one, two, three = group(0), group(1), group(2)
    stage(prepare, one)
    stage(first_product, one)
    stage(prepare, two)
    stage(elementwise, one)
    stage(first_product, two)
    stage(prepare, three)
    steps = jnp.maximum((number + TOGETHER - 1) // TOGETHER, 3)
    three, two, one = lax.fori_loop(3, steps, one_step, (three, two, one))
    stage(second_product, one)
    stage(elementwise, two)
    stage(first_product, three)
    stage(second_product, two)
    stage(elementwise, three)
    stage(second_product, three)
    length = length_ref[0]
    elapsed = step_ref[0].astype(jnp.float32) * length
    strength = BLAST_STRENGTH * jnp.exp(jnp.full((1, PB), -elapsed / DECAY_TIME, jnp.float32))
    for block in range(BLK_DEV):
        fields = all_ref[tile * CHUNK + 1 + block]
        columns = pl.ds(block * PB, PB)
        moments = total[block, 0, 0:4] + total[block, 0, 4:8]
        growth = -(total[block, 1, 0:1] + total[block, 1, 4:5])
        relative = fields[0:3] + 1.0
        spread_sq = jnp.sum(relative * relative, axis=0, keepdims=True) + 1.0
        source = strength * relative / (spread_sq * jnp.sqrt(spread_sq))
        pushed = (fields - centre[block])[0:3] * moments[0:1] - moments[1:4]
        forcing = pushed + source
        velocity = fields[3:6] + length * forcing
        position = fields[0:3] + length * velocity
        density = fields[6:7] + length * growth
        rates_ref[:, columns] = jnp.concatenate([growth, forcing], axis=0)
        ahead_ref[:, columns] = jnp.concatenate([position, velocity, density], axis=0)


def rates_of(step_index, time_step, gathered):
    smem = pl.BlockSpec(memory_space=pltpu.SMEM)
    vmem = pl.BlockSpec(memory_space=pltpu.VMEM)
    all_blocks, codes, centre, left, push, rho = gathered
    return pl.pallas_call(
        rates_kernel,
        out_shape=(
            jax.ShapeDtypeStruct((4, BLK_DEV * PB), jnp.float32),
            jax.ShapeDtypeStruct((7, BLK_DEV * PB), jnp.float32),
        ),
        in_specs=[smem, smem] + [vmem] * 6,
        out_specs=(vmem, vmem),
        scratch_shapes=[
            pltpu.VMEM((BLK_DEV + 1, 2, 8, PB), jnp.float32),
            pltpu.VMEM((TOGETHER, 64, 2 * PB), jnp.bfloat16),
            pltpu.VMEM((TOGETHER, PB, 2 * PB), jnp.float32),
            pltpu.VMEM((TOGETHER, 2 * PB, 2 * PB), jnp.bfloat16),
            pltpu.VMEM((3, TOGETHER, 16, 2 * PB), jnp.bfloat16),
            pltpu.VMEM((2, TOGETHER, 8, PB), jnp.float32),
            pltpu.SMEM((8, PB), jnp.int32),
            pltpu.SemaphoreType.DMA,
        ],
        compiler_params=pltpu.CompilerParams(vmem_limit_bytes=16 * 2**20),
        name="tile_rates",
    )(step_index, time_step, codes, all_blocks, centre, left, push, rho)


def on_device(particles, halo_up, halo_down, tile_first, tile_second, tile_live, step_index, time_step):
    mine = jnp.transpose(particles.reshape(8, BLK_DEV, PB), (1, 0, 2))
    gathered = gather(halo_up, halo_down, tile_first, tile_second, tile_live, mine)
    return rates_of(step_index, time_step, gathered)


def solution(mesh):
    placed = (
        P(None, ("slab", "tile")),
        P(("slab", "tile")),
        P(("slab", "tile")),
        P("slab", "tile"),
        P("slab", "tile"),
        P("slab", "tile"),
        P(),
        P(),
    )
    return jax.shard_map(
        on_device,
        mesh=mesh,
        in_specs=placed,
        out_specs=(P(None, ("slab", "tile")), P(None, ("slab", "tile"))),
        check_vma=False,
    )
```

```python
import heapq
import itertools

import jax
import jax.numpy as jnp
from jax import lax
from jax.experimental import pallas as pl
from jax.experimental.pallas import tpu as pltpu
from jax.sharding import PartitionSpec as P

PB = 128
BLK_DEV = 16
N_SLAB = 16
X, Z = 4, 8
N_TILE = X * Z
CHUNK = 1 + BLK_DEV + 2
NO_TILE = BLK_DEV * 1024

SMOOTHING = 1.0
KERNEL_NORM = 21.0 / (16.0 * 3.141592653589793)
SOUND_SPEED = 10.0
STIFFNESS = SOUND_SPEED * SOUND_SPEED / 7.0
VISCOSITY = 0.1
BLAST_STRENGTH = 8.0
DECAY_TIME = 8.0

MESH = pl.DeviceIdType.MESH

PARTS = (
    dict(first="x", x2="-", z4="-", lo=13, hi=19, at=1.9),
    dict(first="z", x2="-", z4="+", lo=7, hi=13, at=0.1),
    dict(first="z", x2="+", z4="-", lo=0, hi=7, at=0.4),
)
BLOCK_US = 4096 / 46.5e3
HOP_US = 3.0


def tree(part):
    x_from = {1: (0, "x+"), 3: (0, "x-"), 2: (1, "x+") if part["x2"] == "+" else (3, "x-")}
    z_from = {1: (0, "z+"), 2: (1, "z+"), 3: (2, "z+"), 7: (0, "z-"), 6: (7, "z-"), 5: (6, "z-")}
    z_from[4] = (3, "z+") if part["z4"] == "+" else (5, "z-")
    children = {}
    for dx, dz in itertools.product(range(X), range(Z)):
        if (dx, dz) == (0, 0):
            continue
        along_z = dz != 0 if part["first"] == "x" else dx == 0
        if along_z:
            parent, way = (dx, z_from[dz][0]), z_from[dz][1]
        else:
            parent, way = (x_from[dx][0], dz), x_from[dx][1]
        children.setdefault(parent, []).append((way, (dx, dz)))
    return children


def schedule():
    trees = [tree(part) for part in PARTS]

    def depth(index, node):
        return max([0] + [1 + depth(index, child) for _, child in trees[index].get(node, [])])

    free = {"x+": 0.0, "x-": 0.0, "z+": 0.0, "z-": 0.0}
    ticket = itertools.count()
    events = [(part["at"], next(ticket), index, (0, 0)) for index, part in enumerate(PARTS)]
    heapq.heapify(events)
    steps = []
    while events:
        now, _, index, node = heapq.heappop(events)
        sends = sorted(trees[index].get(node, []), key=lambda item: -depth(index, item[1]))
        steps.append((index, node, sends))
        blocks = PARTS[index]["hi"] - PARTS[index]["lo"]
        for way, child in sends:
            done = max(now, free[way]) + blocks * BLOCK_US
            free[way] = done
            heapq.heappush(events, (done + HOP_US, next(ticket), index, child))
    return steps


STEPS = schedule()
LEAVES = {(index, node) for index, node, sends in STEPS if not sends}
EARLY = 8


def gather_kernel(up_ref, down_ref, first_ref, second_ref, live_ref, mine_ref,
                  all_ref, codes_ref, centre_ref, left_ref, push_ref, rho_ref,
                  own, rim, slots, fetch_sem, rim_send, rim_recv, send_sem, recv_sem, leaf_sem):
    slab = lax.axis_index("slab")
    tile = lax.axis_index("tile")
    x, z = tile // Z, tile % Z
    above = lax.rem(slab + 1, N_SLAB)
    below = lax.rem(slab + N_SLAB - 1, N_SLAB)
    beside = {
        "x+": lax.rem(x + 1, X) * Z + z,
        "x-": lax.rem(x + X - 1, X) * Z + z,
        "z+": x * Z + lax.rem(z + 1, Z),
        "z-": x * Z + lax.rem(z + Z - 1, Z),
    }
    row = iota((8, PB), 0)

    def held(origin, low, high):
        return all_ref.at[pl.ds(origin * CHUNK + low, high - low)]

    place = pltpu.make_async_copy(mine_ref, held(tile, 1, 1 + BLK_DEV), fetch_sem.at[0])
    load = pltpu.make_async_copy(mine_ref, own, fetch_sem.at[1])
    fetch = [
        pltpu.make_async_copy(ref, slots.at[index], fetch_sem.at[2 + index])
        for index, ref in enumerate((first_ref, second_ref, live_ref))
    ]
    place.start()
    for copy in fetch:
        copy.start()
    load.start()
    barrier = pltpu.get_barrier_semaphore()
    for way in beside:
        pl.semaphore_signal(barrier, inc=1, device_id=(slab, beside[way]), device_id_type=MESH)
    pl.semaphore_signal(barrier, inc=1, device_id=(above, tile), device_id_type=MESH)
    pl.semaphore_signal(barrier, inc=1, device_id=(below, tile), device_id_type=MESH)
    pl.semaphore_wait(barrier, 6)

    def rim_copy(side):
        return pltpu.make_async_remote_copy(
            src_ref=rim.at[pl.ds(side, 1)],
            dst_ref=held(tile, 1 + BLK_DEV + side, 2 + BLK_DEV + side),
            send_sem=rim_send.at[side],
            recv_sem=rim_recv.at[side],
            device_id=(above if side == 0 else below, tile),
            device_id_type=MESH,
        )

    def pass_on(where, signal, way, source=None):
        return pltpu.make_async_remote_copy(
            src_ref=where if source is None else source,
            dst_ref=where,
            send_sem=send_sem,
            recv_sem=signal,
            device_id=(slab, beside[way]),
            device_id_type=MESH,
        )

    from_x = [lax.rem(x + X - step, X) * (Z * CHUNK) for step in range(X)]
    from_z = [lax.rem(z + Z - step, Z) * CHUNK for step in range(Z)]

    def piece(index, node):
        low, high = PARTS[index]["lo"], PARTS[index]["hi"]
        return all_ref.at[pl.ds(from_x[node[0]] + from_z[node[1]] + low, high - low)]

    def arrival(index, node):
        if (index, node) in LEAVES:
            return leaf_sem.at[0 if PARTS[index]["lo"] == 0 else 1]
        return recv_sem.at[index * N_TILE + node[0] * Z + node[1]]

    def one_pair(pair, carry):
        for block in (2 * pair, 2 * pair + 1):
            middle, side = receiver(own[block], row)
            centre_ref[block] = middle
            left_ref[block] = side.astype(jnp.bfloat16)
            push_ref[block] = jnp.broadcast_to(side[:, 56:57], (PB, PB))
            rho_ref[block] = jnp.broadcast_to(side[:, 57:58], (PB, PB))
        return carry

    rims = [rim_copy(0), rim_copy(1)]
    for index, node, sends in STEPS:
        part = PARTS[index]
        if node == (0, 0) and part["lo"] > 0 and part["hi"] <= 1 + BLK_DEV:
            for way, child in sends:
                source = mine_ref.at[pl.ds(part["lo"] - 1, part["hi"] - part["lo"])]
                pass_on(piece(index, node), arrival(index, child), way, source).start()
    for copy in fetch:
        copy.wait()
    all_ref[tile * CHUNK] = jnp.where(
        row == 0, slots[0], jnp.where(row == 1, slots[1], jnp.where(row == 2, slots[2], 0))
    ).astype(jnp.float32)
    load.wait()
    rim[0] = own[up_ref[0]]
    rim[1] = own[down_ref[0]]
    lax.fori_loop(0, 1, one_pair, 0)
    for copy in rims:
        copy.start()
    place.wait()
    for index, node, sends in STEPS:
        if (index, node) in LEAVES:
            continue
        part = PARTS[index]
        if node == (0, 0) and part["lo"] > 0 and part["hi"] <= 1 + BLK_DEV:
            continue
        where = piece(index, node)
        if node != (0, 0):
            pass_on(where, arrival(index, node), "x+").wait_recv()
        elif part["hi"] == CHUNK:
            lax.fori_loop(1, EARLY // 2, one_pair, 0)
            for copy in rims:
                copy.wait_recv()
        for way, child in sends:
            pass_on(where, arrival(index, child), way).start()
    lax.fori_loop(EARLY // 2, BLK_DEV // 2, one_pair, 0)
    centre_ref[BLK_DEV] = jnp.zeros((8, PB), jnp.float32)
    left_ref[BLK_DEV] = jnp.zeros((PB, 64), jnp.bfloat16)
    push_ref[BLK_DEV] = jnp.zeros((PB, PB), jnp.float32)
    rho_ref[BLK_DEV] = jnp.full((PB, PB), -1.0, jnp.float32)
    listed, other = (sum(PARTS[index]["hi"] - PARTS[index]["lo"] for index, _ in LEAVES
                         if (PARTS[index]["lo"] == 0) == first) for first in (True, False))
    pass_on(all_ref.at[pl.ds(0, listed)], leaf_sem.at[0], "x+").wait_recv()
    codes_ref[...] = choose_tiles(all_ref, slab, tile)
    pass_on(all_ref.at[pl.ds(0, other)], leaf_sem.at[1], "x+").wait_recv()
    for copy in rims:
        copy.wait_send()
    pass_on(all_ref.at[pl.ds(0, (N_TILE - 1) * CHUNK)], leaf_sem.at[0], "x+").wait_send()


def gather(halo_up, halo_down, tile_first, tile_second, tile_live, mine):
    smem = pl.BlockSpec(memory_space=pltpu.SMEM)
    hbm = pl.BlockSpec(memory_space=pltpu.HBM)
    vmem = pl.BlockSpec(memory_space=pltpu.VMEM)
    in_hbm = [
        pltpu.with_memory_space_constraint(array, pltpu.HBM)
        for array in (tile_first, tile_second, tile_live, mine)
    ]
    return pl.pallas_call(
        gather_kernel,
        out_shape=(
            jax.ShapeDtypeStruct((N_TILE * CHUNK, 8, PB), jnp.float32),
            jax.ShapeDtypeStruct((8, PB), jnp.int32),
            jax.ShapeDtypeStruct((BLK_DEV + 1, 8, PB), jnp.float32),
            jax.ShapeDtypeStruct((BLK_DEV + 1, PB, 64), jnp.bfloat16),
            jax.ShapeDtypeStruct((BLK_DEV + 1, PB, PB), jnp.float32),
            jax.ShapeDtypeStruct((BLK_DEV + 1, PB, PB), jnp.float32),
        ),
        in_specs=[smem, smem, hbm, hbm, hbm, hbm],
        out_specs=(vmem,) * 6,
        scratch_shapes=[
            pltpu.VMEM((BLK_DEV, 8, PB), jnp.float32),
            pltpu.VMEM((2, 8, PB), jnp.float32),
            pltpu.VMEM((3, 1, PB), jnp.int32),
            pltpu.SemaphoreType.DMA((5,)),
            pltpu.SemaphoreType.DMA((2,)),
            pltpu.SemaphoreType.DMA((2,)),
            pltpu.SemaphoreType.DMA,
            pltpu.SemaphoreType.DMA((len(PARTS) * N_TILE,)),
            pltpu.SemaphoreType.DMA((2,)),
        ],
        compiler_params=pltpu.CompilerParams(collective_id=0, has_side_effects=True, vmem_limit_bytes=16 * 2**20),
        name="gather_blocks",
    )(halo_up, halo_down, *in_hbm)


def iota(shape, axis):
    return lax.broadcasted_iota(jnp.int32, shape, axis)


def choose_tiles(all_ref, slab, tile):
    first, second, live = (
        jnp.concatenate(
            [all_ref[origin * CHUNK, pl.ds(place, 1)] for origin in range(N_TILE)], axis=0
        ).astype(jnp.int32)
        for place in range(3)
    )
    missing = ((slab == 0) & (second >= 512) & (second < 544)) | ((slab == N_SLAB - 1) & (second >= 544))
    wanted = ((first >> 4) == tile) & (live == 1) & jnp.logical_not(missing)
    source = jnp.where(
        second < 512,
        (second >> 4) * CHUNK + 1 + (second & 15),
        ((second - 512) & 31) * CHUNK + 1 + BLK_DEV + ((second - 512) >> 5),
    )
    code = ((first & 15) * 1024 + source).astype(jnp.float32)
    ones = jnp.where(wanted, 1.0, 0.0)
    upto = (iota((PB, PB), 0) <= iota((PB, PB), 1)).astype(jnp.float32)
    within = jnp.dot(ones, upto, preferred_element_type=jnp.float32)
    earlier = (iota((N_TILE, N_TILE), 1) < iota((N_TILE, N_TILE), 0)).astype(jnp.float32)
    before = jnp.dot(earlier, within, preferred_element_type=jnp.float32)[:, PB - 1 :]
    place = jnp.where(wanted, (before + within).astype(jnp.int32) - 1, -1)
    target = iota((PB, PB), 0)
    chosen = jnp.zeros((PB, PB), jnp.float32)
    for row in range(N_TILE):
        chosen = jnp.where(place[row : row + 1, :] == target, code[row : row + 1, :], chosen)
    codes = lax.dot_general(
        jnp.ones((8, PB), jnp.float32), chosen, (((1,), (1,)), ((), ())),
        precision=lax.Precision.HIGHEST, preferred_element_type=jnp.float32,
    )
    count = jnp.sum(before[N_TILE - 1 :, :] + within[N_TILE - 1 :, PB - 1 :])
    row = iota((8, PB), 0)
    codes = jnp.where((row == 0) & (iota((8, PB), 1).astype(jnp.float32) < count), codes, float(NO_TILE))
    return jnp.where(row == 2, count, codes).astype(jnp.int32)


def shifted(rows, up):
    return pltpu.roll(rows, (8 - up) % 8, 0)


def parts_of(value):
    high = value.astype(jnp.bfloat16).astype(jnp.float32)
    rest = value - high
    middle = rest.astype(jnp.bfloat16).astype(jnp.float32)
    return high, middle, rest - middle


def squares_and_products(centred):
    squares = centred * centred
    products = centred * shifted(centred, 3)
    return (
        squares + shifted(squares, 1) + shifted(squares, 2),
        products + shifted(products, 1) + shifted(products, 2),
    )


def pressure_term(density):
    squared = density * density
    return STIFFNESS * (squared * squared * squared * density - 1.0) / squared


def receiver(fields, row):
    centre = jnp.where(row < 6, jnp.broadcast_to(fields[:, 0:1], (8, PB)), 0.0)
    centred = fields - centre
    squares, products = squares_and_products(centred)
    plain = jnp.where(row < 6, centred, jnp.where(row == 6, 1.0, 0.0))
    high, middle, low = parts_of(plain)
    extra = jnp.zeros((8, PB), jnp.float32)
    for place, value in enumerate(parts_of(squares) + parts_of(products)):
        extra = jnp.where(row == place, value if place == 0 else shifted(value, 8 - place), extra)
    pressure = pressure_term(fields)
    columns = jnp.where(row == 0, shifted(pressure, 6), jnp.where(row == 1, shifted(-0.5 * fields, 5), 0.0))
    return centre, jnp.concatenate([high, high, middle, middle, high, low, extra, columns], axis=0).T


def actor_side(centred, row):
    squares, products = squares_and_products(centred)
    for_square = jnp.where(row < 3, -2.0 * centred, jnp.where(row == 6, shifted(squares, 2), 0.0))
    for_approach = jnp.where(
        row < 3, -shifted(centred, 3), jnp.where(row < 6, -shifted(centred, 5), jnp.where(row == 6, shifted(products, 2), 0.0))
    )
    sides = []
    for value, ones in ((for_square, row < 3), (for_approach, (row >= 3) & (row < 6))):
        high, middle, low = parts_of(value)
        extra = jnp.where(ones, 1.0, 0.0)
        sides.append(
            jnp.concatenate([high, middle, high, middle, low, high, extra, jnp.zeros((8, PB), jnp.float32)], axis=0)
        )
    return jnp.concatenate(sides, axis=1).astype(jnp.bfloat16)


TOGETHER = 3


def rates_kernel(step_ref, length_ref, codes, all_ref, centre, left, push, rho, rates_ref, ahead_ref,
                 total, right, squares, factor, moment, acts, plan, plan_sem):
    tile = lax.axis_index("tile")
    row = iota((8, PB), 0)
    copy = pltpu.make_async_copy(codes, plan, plan_sem)
    copy.start()
    total[...] = jnp.zeros_like(total)
    copy.wait()
    number = plan[2, 0]

    def prepare(code, slot):
        fields = all_ref[code & 1023]
        centred = fields - centre[code >> 10]
        right[slot] = actor_side(centred, row)
        mass = jnp.broadcast_to(fields[7:8] * (5.0 * KERNEL_NORM / 8.0), (8, PB))
        weighted = jnp.where(row == 0, 1.0, shifted(centred, 7)) * mass
        high = weighted.astype(jnp.bfloat16).astype(jnp.float32)
        both = jnp.where(row < 4, high, shifted(weighted - high, 4))
        both = jnp.concatenate([both, jnp.zeros((8, PB), jnp.float32)], axis=0).astype(jnp.bfloat16)
        moment[0, slot] = jnp.concatenate([both, both], axis=1)
        acts[0, slot] = jnp.where(row == 6, pressure_term(fields), -0.5 * shifted(fields, 7))

    def first_product(code, slot):
        squares[slot] = jnp.dot(left[code >> 10], right[slot], preferred_element_type=jnp.float32)
        moment[1, slot] = moment[0, slot]
        acts[1, slot] = acts[0, slot]

    def elementwise(code, slot):
        a = code >> 10
        act_push = jnp.broadcast_to(acts[1, slot, 6:7], (16, PB))
        act_rho = jnp.broadcast_to(acts[1, slot, 7:8], (16, PB))
        for low in range(0, PB, 16):
            rows = pl.ds(low, 16)
            dist_sq = jnp.maximum(squares[slot, rows, 0:PB], 1e-30)
            approach = squares[slot, rows, PB : 2 * PB]
            reach = jnp.maximum(2.0 - dist_sq * lax.rsqrt(dist_sq), 0.0)
            weight = reach * reach * reach
            growth = approach * weight
            damping = jnp.minimum(approach, 0.0) / ((dist_sq + 0.01) * (rho[a, rows] + act_rho))
            pressing = (push[a, rows] + act_push + damping) * weight
            for place, value in ((0, pressing), (PB, growth)):
                high = value.astype(jnp.bfloat16)
                lower = (value - high.astype(jnp.float32)).astype(jnp.bfloat16)
                factor[slot, pl.ds(place + low, 16), 0:PB] = high
                factor[slot, pl.ds(place + low, 16), PB : 2 * PB] = lower
        moment[2, slot] = moment[1, slot]

    def second_product(code, slot):
        a = code >> 10
        sums = lax.dot_general(
            moment[2, slot], factor[slot], (((1,), (1,)), ((), ())), preferred_element_type=jnp.float32
        )
        total[a, 0] += sums[0:8, 0:PB]
        total[a, 1] += sums[0:8, PB : 2 * PB]

    def group(step):
        return [plan[(TOGETHER * step + slot) >> 7, (TOGETHER * step + slot) & 127] for slot in range(TOGETHER)]

    def stage(work, codes_now):
        for slot in range(TOGETHER):
            work(codes_now[slot], slot)

    def one_step(step, stages):
        made, multiplied, weighed = stages
        fresh = group(step)
        stage(second_product, weighed)
        stage(elementwise, multiplied)
        stage(first_product, made)
        stage(prepare, fresh)
        return fresh, made, multiplied

    one, two, three = group(0), group(1), group(2)
    stage(prepare, one)
    stage(first_product, one)
    stage(prepare, two)
    stage(elementwise, one)
    stage(first_product, two)
    stage(prepare, three)
    steps = jnp.maximum((number + TOGETHER - 1) // TOGETHER, 3)
    three, two, one = lax.fori_loop(3, steps, one_step, (three, two, one))
    stage(second_product, one)
    stage(elementwise, two)
    stage(first_product, three)
    stage(second_product, two)
    stage(elementwise, three)
    stage(second_product, three)
    length = length_ref[0]
    elapsed = step_ref[0].astype(jnp.float32) * length
    strength = BLAST_STRENGTH * jnp.exp(jnp.full((1, PB), -elapsed / DECAY_TIME, jnp.float32))
    for block in range(BLK_DEV):
        fields = all_ref[tile * CHUNK + 1 + block]
        columns = pl.ds(block * PB, PB)
        moments = total[block, 0, 0:4] + total[block, 0, 4:8]
        growth = -(total[block, 1, 0:1] + total[block, 1, 4:5])
        relative = fields[0:3] + 1.0
        spread_sq = jnp.sum(relative * relative, axis=0, keepdims=True) + 1.0
        source = strength * relative / (spread_sq * jnp.sqrt(spread_sq))
        pushed = (fields - centre[block])[0:3] * moments[0:1] - moments[1:4]
        forcing = pushed + source
        velocity = fields[3:6] + length * forcing
        position = fields[0:3] + length * velocity
        density = fields[6:7] + length * growth
        rates_ref[:, columns] = jnp.concatenate([growth, forcing], axis=0)
        ahead_ref[:, columns] = jnp.concatenate([position, velocity, density], axis=0)


def rates_of(step_index, time_step, gathered):
    smem = pl.BlockSpec(memory_space=pltpu.SMEM)
    vmem = pl.BlockSpec(memory_space=pltpu.VMEM)
    all_blocks, codes, centre, left, push, rho = gathered
    return pl.pallas_call(
        rates_kernel,
        out_shape=(
            jax.ShapeDtypeStruct((4, BLK_DEV * PB), jnp.float32),
            jax.ShapeDtypeStruct((7, BLK_DEV * PB), jnp.float32),
        ),
        in_specs=[smem, smem] + [vmem] * 6,
        out_specs=(vmem, vmem),
        scratch_shapes=[
            pltpu.VMEM((BLK_DEV + 1, 2, 8, PB), jnp.float32),
            pltpu.VMEM((TOGETHER, 64, 2 * PB), jnp.bfloat16),
            pltpu.VMEM((TOGETHER, PB, 2 * PB), jnp.float32),
            pltpu.VMEM((TOGETHER, 2 * PB, 2 * PB), jnp.bfloat16),
            pltpu.VMEM((3, TOGETHER, 16, 2 * PB), jnp.bfloat16),
            pltpu.VMEM((2, TOGETHER, 8, PB), jnp.float32),
            pltpu.SMEM((8, PB), jnp.int32),
            pltpu.SemaphoreType.DMA,
        ],
        compiler_params=pltpu.CompilerParams(vmem_limit_bytes=16 * 2**20),
        name="tile_rates",
    )(step_index, time_step, codes, all_blocks, centre, left, push, rho)


def on_device(particles, halo_up, halo_down, tile_first, tile_second, tile_live, step_index, time_step):
    mine = jnp.transpose(particles.reshape(8, BLK_DEV, PB), (1, 0, 2))
    gathered = gather(halo_up, halo_down, tile_first, tile_second, tile_live, mine)
    return rates_of(step_index, time_step, gathered)


def solution(mesh):
    placed = (
        P(None, ("slab", "tile")),
        P(("slab", "tile")),
        P(("slab", "tile")),
        P("slab", "tile"),
        P("slab", "tile"),
        P("slab", "tile"),
        P(),
        P(),
    )
    return jax.shard_map(
        on_device,
        mesh=mesh,
        in_specs=placed,
        out_specs=(P(None, ("slab", "tile")), P(None, ("slab", "tile"))),
        check_vma=False,
    )
```

```python
import heapq
import itertools

import jax
import jax.numpy as jnp
from jax import lax
from jax.experimental import pallas as pl
from jax.experimental.pallas import tpu as pltpu
from jax.sharding import PartitionSpec as P

PB = 128
BLK_DEV = 16
N_SLAB = 16
X, Z = 4, 8
N_TILE = X * Z
CHUNK = 1 + BLK_DEV + 2
NO_TILE = BLK_DEV * 1024

SMOOTHING = 1.0
KERNEL_NORM = 21.0 / (16.0 * 3.141592653589793)
SOUND_SPEED = 10.0
STIFFNESS = SOUND_SPEED * SOUND_SPEED / 7.0
VISCOSITY = 0.1
BLAST_STRENGTH = 8.0
DECAY_TIME = 8.0

MESH = pl.DeviceIdType.MESH

PARTS = (
    dict(first="x", x2="-", z4="-", lo=13, hi=19, at=1.9),
    dict(first="z", x2="-", z4="+", lo=7, hi=13, at=0.1),
    dict(first="z", x2="+", z4="-", lo=0, hi=7, at=0.4),
)
BLOCK_US = 4096 / 46.5e3
HOP_US = 3.0


def tree(part):
    x_from = {1: (0, "x+"), 3: (0, "x-"), 2: (1, "x+") if part["x2"] == "+" else (3, "x-")}
    z_from = {1: (0, "z+"), 2: (1, "z+"), 3: (2, "z+"), 7: (0, "z-"), 6: (7, "z-"), 5: (6, "z-")}
    z_from[4] = (3, "z+") if part["z4"] == "+" else (5, "z-")
    children = {}
    for dx, dz in itertools.product(range(X), range(Z)):
        if (dx, dz) == (0, 0):
            continue
        along_z = dz != 0 if part["first"] == "x" else dx == 0
        if along_z:
            parent, way = (dx, z_from[dz][0]), z_from[dz][1]
        else:
            parent, way = (x_from[dx][0], dz), x_from[dx][1]
        children.setdefault(parent, []).append((way, (dx, dz)))
    return children


def schedule():
    trees = [tree(part) for part in PARTS]

    def depth(index, node):
        return max([0] + [1 + depth(index, child) for _, child in trees[index].get(node, [])])

    free = {"x+": 0.0, "x-": 0.0, "z+": 0.0, "z-": 0.0}
    ticket = itertools.count()
    events = [(part["at"], next(ticket), index, (0, 0)) for index, part in enumerate(PARTS)]
    heapq.heapify(events)
    steps = []
    while events:
        now, _, index, node = heapq.heappop(events)
        sends = sorted(trees[index].get(node, []), key=lambda item: -depth(index, item[1]))
        steps.append((index, node, sends))
        blocks = PARTS[index]["hi"] - PARTS[index]["lo"]
        for way, child in sends:
            done = max(now, free[way]) + blocks * BLOCK_US
            free[way] = done
            heapq.heappush(events, (done + HOP_US, next(ticket), index, child))
    return steps


STEPS = schedule()
LEAVES = {(index, node) for index, node, sends in STEPS if not sends}
EARLY = 8


def gather_kernel(up_ref, down_ref, first_ref, second_ref, live_ref, mine_ref,
                  all_ref, codes_ref, centre_ref, left_ref, push_ref, rho_ref,
                  own, rim, slots, chosen, fetch_sem, rim_send, rim_recv, send_sem, recv_sem, leaf_sem):
    slab = lax.axis_index("slab")
    tile = lax.axis_index("tile")
    x, z = tile // Z, tile % Z
    above = lax.rem(slab + 1, N_SLAB)
    below = lax.rem(slab + N_SLAB - 1, N_SLAB)
    beside = {
        "x+": lax.rem(x + 1, X) * Z + z,
        "x-": lax.rem(x + X - 1, X) * Z + z,
        "z+": x * Z + lax.rem(z + 1, Z),
        "z-": x * Z + lax.rem(z + Z - 1, Z),
    }
    row = iota((8, PB), 0)

    def held(origin, low, high):
        return all_ref.at[pl.ds(origin * CHUNK + low, high - low)]

    place = pltpu.make_async_copy(mine_ref, held(tile, 1, 1 + BLK_DEV), fetch_sem.at[0])
    load = pltpu.make_async_copy(mine_ref, own, fetch_sem.at[1])
    fetch = [
        pltpu.make_async_copy(ref, slots.at[index], fetch_sem.at[2 + index])
        for index, ref in enumerate((first_ref, second_ref, live_ref))
    ]
    barrier = pltpu.get_barrier_semaphore()
    for way in beside:
        pl.semaphore_signal(barrier, inc=1, device_id=(slab, beside[way]), device_id_type=MESH)
    pl.semaphore_signal(barrier, inc=1, device_id=(above, tile), device_id_type=MESH)
    pl.semaphore_signal(barrier, inc=1, device_id=(below, tile), device_id_type=MESH)
    place.start()
    for copy in fetch:
        copy.start()
    load.start()
    pl.semaphore_wait(barrier, 6)

    def rim_copy(side):
        return pltpu.make_async_remote_copy(
            src_ref=rim.at[pl.ds(side, 1)],
            dst_ref=held(tile, 1 + BLK_DEV + side, 2 + BLK_DEV + side),
            send_sem=rim_send.at[side],
            recv_sem=rim_recv.at[side],
            device_id=(above if side == 0 else below, tile),
            device_id_type=MESH,
        )

    def pass_on(where, signal, way, source=None):
        return pltpu.make_async_remote_copy(
            src_ref=where if source is None else source,
            dst_ref=where,
            send_sem=send_sem,
            recv_sem=signal,
            device_id=(slab, beside[way]),
            device_id_type=MESH,
        )

    from_x = [lax.rem(x + X - step, X) * (Z * CHUNK) for step in range(X)]
    from_z = [lax.rem(z + Z - step, Z) * CHUNK for step in range(Z)]

    def piece(index, node):
        low, high = PARTS[index]["lo"], PARTS[index]["hi"]
        return all_ref.at[pl.ds(from_x[node[0]] + from_z[node[1]] + low, high - low)]

    def arrival(index, node):
        if (index, node) in LEAVES:
            return leaf_sem.at[0 if PARTS[index]["lo"] == 0 else 1]
        return recv_sem.at[index * N_TILE + node[0] * Z + node[1]]

    def one_pair(pair, carry):
        for block in (2 * pair, 2 * pair + 1):
            middle, side = receiver(own[block], row)
            centre_ref[block] = middle
            left_ref[block] = side.astype(jnp.bfloat16)
            push_ref[block] = jnp.broadcast_to(side[:, 56:57], (PB, PB))
            rho_ref[block] = jnp.broadcast_to(side[:, 57:58], (PB, PB))
        return carry

    rims = [rim_copy(0), rim_copy(1)]
    for index, node, sends in STEPS:
        part = PARTS[index]
        if node == (0, 0) and part["lo"] > 0 and part["hi"] <= 1 + BLK_DEV:
            for way, child in sends:
                source = mine_ref.at[pl.ds(part["lo"] - 1, part["hi"] - part["lo"])]
                pass_on(piece(index, node), arrival(index, child), way, source).start()
    for copy in fetch:
        copy.wait()
    all_ref[tile * CHUNK] = jnp.where(
        row == 0, slots[0], jnp.where(row == 1, slots[1], jnp.where(row == 2, slots[2], 0))
    ).astype(jnp.float32)
    load.wait()
    rim[0] = own[up_ref[0]]
    rim[1] = own[down_ref[0]]
    lax.fori_loop(0, 1, one_pair, 0)
    for copy in rims:
        copy.start()
    place.wait()
    for index, node, sends in STEPS:
        if (index, node) in LEAVES:
            continue
        part = PARTS[index]
        if node == (0, 0) and part["lo"] > 0 and part["hi"] <= 1 + BLK_DEV:
            continue
        where = piece(index, node)
        if node != (0, 0):
            pass_on(where, arrival(index, node), "x+").wait_recv()
        elif part["hi"] == CHUNK:
            lax.fori_loop(1, EARLY // 2, one_pair, 0)
            for copy in rims:
                copy.wait_recv()
        for way, child in sends:
            pass_on(where, arrival(index, child), way).start()
    lax.fori_loop(EARLY // 2, BLK_DEV // 2, one_pair, 0)
    centre_ref[BLK_DEV] = jnp.zeros((8, PB), jnp.float32)
    left_ref[BLK_DEV] = jnp.zeros((PB, 64), jnp.bfloat16)
    push_ref[BLK_DEV] = jnp.zeros((PB, PB), jnp.float32)
    rho_ref[BLK_DEV] = jnp.full((PB, PB), -1.0, jnp.float32)
    listed, other = (sum(PARTS[index]["hi"] - PARTS[index]["lo"] for index, _ in LEAVES
                         if (PARTS[index]["lo"] == 0) == first) for first in (True, False))
    pass_on(all_ref.at[pl.ds(0, listed)], leaf_sem.at[0], "x+").wait_recv()
    chosen[...] = choose_tiles(all_ref, slab, tile)
    hand = pltpu.make_async_copy(chosen, codes_ref, fetch_sem.at[5])
    hand.start()
    pass_on(all_ref.at[pl.ds(0, other)], leaf_sem.at[1], "x+").wait_recv()
    hand.wait()
    for copy in rims:
        copy.wait_send()
    pass_on(all_ref.at[pl.ds(0, (N_TILE - 1) * CHUNK)], leaf_sem.at[0], "x+").wait_send()


def gather(halo_up, halo_down, tile_first, tile_second, tile_live, mine):
    smem = pl.BlockSpec(memory_space=pltpu.SMEM)
    hbm = pl.BlockSpec(memory_space=pltpu.HBM)
    vmem = pl.BlockSpec(memory_space=pltpu.VMEM)
    in_hbm = [
        pltpu.with_memory_space_constraint(array, pltpu.HBM)
        for array in (tile_first, tile_second, tile_live, mine)
    ]
    return pl.pallas_call(
        gather_kernel,
        out_shape=(
            jax.ShapeDtypeStruct((N_TILE * CHUNK, 8, PB), jnp.float32),
            jax.ShapeDtypeStruct((8, PB), jnp.int32),
            jax.ShapeDtypeStruct((BLK_DEV + 1, 8, PB), jnp.float32),
            jax.ShapeDtypeStruct((BLK_DEV + 1, PB, 64), jnp.bfloat16),
            jax.ShapeDtypeStruct((BLK_DEV + 1, PB, PB), jnp.float32),
            jax.ShapeDtypeStruct((BLK_DEV + 1, PB, PB), jnp.float32),
        ),
        in_specs=[smem, smem, hbm, hbm, hbm, hbm],
        out_specs=(vmem, pl.BlockSpec(memory_space=pltpu.SMEM)) + (vmem,) * 4,
        scratch_shapes=[
            pltpu.VMEM((BLK_DEV, 8, PB), jnp.float32),
            pltpu.VMEM((2, 8, PB), jnp.float32),
            pltpu.VMEM((3, 1, PB), jnp.int32),
            pltpu.VMEM((8, PB), jnp.int32),
            pltpu.SemaphoreType.DMA((6,)),
            pltpu.SemaphoreType.DMA((2,)),
            pltpu.SemaphoreType.DMA((2,)),
            pltpu.SemaphoreType.DMA,
            pltpu.SemaphoreType.DMA((len(PARTS) * N_TILE,)),
            pltpu.SemaphoreType.DMA((2,)),
        ],
        compiler_params=pltpu.CompilerParams(collective_id=0, has_side_effects=True, vmem_limit_bytes=16 * 2**20),
        name="gather_blocks",
    )(halo_up, halo_down, *in_hbm)


def iota(shape, axis):
    return lax.broadcasted_iota(jnp.int32, shape, axis)


def choose_tiles(all_ref, slab, tile):
    first, second, live = (
        jnp.concatenate(
            [all_ref[origin * CHUNK, pl.ds(place, 1)] for origin in range(N_TILE)], axis=0
        ).astype(jnp.int32)
        for place in range(3)
    )
    missing = ((slab == 0) & (second >= 512) & (second < 544)) | ((slab == N_SLAB - 1) & (second >= 544))
    wanted = ((first >> 4) == tile) & (live == 1) & jnp.logical_not(missing)
    source = jnp.where(
        second < 512,
        (second >> 4) * CHUNK + 1 + (second & 15),
        ((second - 512) & 31) * CHUNK + 1 + BLK_DEV + ((second - 512) >> 5),
    )
    code = ((first & 15) * 1024 + source).astype(jnp.float32)
    ones = jnp.where(wanted, 1.0, 0.0)
    upto = (iota((PB, PB), 0) <= iota((PB, PB), 1)).astype(jnp.float32)
    within = jnp.dot(ones, upto, preferred_element_type=jnp.float32)
    earlier = (iota((N_TILE, N_TILE), 1) < iota((N_TILE, N_TILE), 0)).astype(jnp.float32)
    before = jnp.dot(earlier, within, preferred_element_type=jnp.float32)[:, PB - 1 :]
    place = jnp.where(wanted, (before + within).astype(jnp.int32) - 1, -1)
    target = iota((PB, PB), 0)
    chosen = jnp.zeros((PB, PB), jnp.float32)
    for row in range(N_TILE):
        chosen = jnp.where(place[row : row + 1, :] == target, code[row : row + 1, :], chosen)
    codes = lax.dot_general(
        jnp.ones((8, PB), jnp.float32), chosen, (((1,), (1,)), ((), ())),
        precision=lax.Precision.HIGHEST, preferred_element_type=jnp.float32,
    )
    count = jnp.sum(before[N_TILE - 1 :, :] + within[N_TILE - 1 :, PB - 1 :])
    row = iota((8, PB), 0)
    codes = jnp.where((row == 0) & (iota((8, PB), 1).astype(jnp.float32) < count), codes, float(NO_TILE))
    return jnp.where(row == 2, count, codes).astype(jnp.int32)


def shifted(rows, up):
    return pltpu.roll(rows, (8 - up) % 8, 0)


def parts_of(value):
    high = value.astype(jnp.bfloat16).astype(jnp.float32)
    rest = value - high
    middle = rest.astype(jnp.bfloat16).astype(jnp.float32)
    return high, middle, rest - middle


def squares_and_products(centred):
    squares = centred * centred
    products = centred * shifted(centred, 3)
    return (
        squares + shifted(squares, 1) + shifted(squares, 2),
        products + shifted(products, 1) + shifted(products, 2),
    )


def pressure_term(density):
    squared = density * density
    return STIFFNESS * (squared * squared * squared * density - 1.0) / squared


def receiver(fields, row):
    centre = jnp.where(row < 6, jnp.broadcast_to(fields[:, 0:1], (8, PB)), 0.0)
    centred = fields - centre
    squares, products = squares_and_products(centred)
    plain = jnp.where(row < 6, centred, jnp.where(row == 6, 1.0, 0.0))
    high, middle, low = parts_of(plain)
    extra = jnp.zeros((8, PB), jnp.float32)
    for place, value in enumerate(parts_of(squares) + parts_of(products)):
        extra = jnp.where(row == place, value if place == 0 else shifted(value, 8 - place), extra)
    pressure = pressure_term(fields)
    columns = jnp.where(row == 0, shifted(pressure, 6), jnp.where(row == 1, shifted(-0.5 * fields, 5), 0.0))
    return centre, jnp.concatenate([high, high, middle, middle, high, low, extra, columns], axis=0).T


def actor_side(centred, row):
    squares, products = squares_and_products(centred)
    for_square = jnp.where(row < 3, -2.0 * centred, jnp.where(row == 6, shifted(squares, 2), 0.0))
    for_approach = jnp.where(
        row < 3, -shifted(centred, 3), jnp.where(row < 6, -shifted(centred, 5), jnp.where(row == 6, shifted(products, 2), 0.0))
    )
    sides = []
    for value, ones in ((for_square, row < 3), (for_approach, (row >= 3) & (row < 6))):
        high, middle, low = parts_of(value)
        extra = jnp.where(ones, 1.0, 0.0)
        sides.append(
            jnp.concatenate([high, middle, high, middle, low, high, extra, jnp.zeros((8, PB), jnp.float32)], axis=0)
        )
    return jnp.concatenate(sides, axis=1).astype(jnp.bfloat16)


TOGETHER = 3


def rates_kernel(step_ref, length_ref, plan, all_ref, centre, left, push, rho, rates_ref, ahead_ref,
                 total, right, squares, factor, moment, acts):
    tile = lax.axis_index("tile")
    row = iota((8, PB), 0)
    total[...] = jnp.zeros_like(total)
    number = plan[2, 0]

    def prepare(code, slot):
        fields = all_ref[code & 1023]
        centred = fields - centre[code >> 10]
        right[slot] = actor_side(centred, row)
        mass = jnp.broadcast_to(fields[7:8] * (5.0 * KERNEL_NORM / 8.0), (8, PB))
        weighted = jnp.where(row == 0, 1.0, shifted(centred, 7)) * mass
        high = weighted.astype(jnp.bfloat16).astype(jnp.float32)
        both = jnp.where(row < 4, high, shifted(weighted - high, 4))
        both = jnp.concatenate([both, jnp.zeros((8, PB), jnp.float32)], axis=0).astype(jnp.bfloat16)
        moment[0, slot] = jnp.concatenate([both, both], axis=1)
        acts[0, slot] = jnp.where(row == 6, pressure_term(fields), -0.5 * shifted(fields, 7))

    def first_product(code, slot):
        squares[slot] = jnp.dot(left[code >> 10], right[slot], preferred_element_type=jnp.float32)
        moment[1, slot] = moment[0, slot]
        acts[1, slot] = acts[0, slot]

    def elementwise(code, slot):
        a = code >> 10
        act_push = jnp.broadcast_to(acts[1, slot, 6:7], (16, PB))
        act_rho = jnp.broadcast_to(acts[1, slot, 7:8], (16, PB))
        for low in range(0, PB, 16):
            rows = pl.ds(low, 16)
            dist_sq = jnp.maximum(squares[slot, rows, 0:PB], 1e-30)
            approach = squares[slot, rows, PB : 2 * PB]
            reach = jnp.maximum(2.0 - dist_sq * lax.rsqrt(dist_sq), 0.0)
            weight = reach * reach * reach
            growth = approach * weight
            damping = jnp.minimum(approach, 0.0) / ((dist_sq + 0.01) * (rho[a, rows] + act_rho))
            pressing = (push[a, rows] + act_push + damping) * weight
            for place, value in ((0, pressing), (PB, growth)):
                high = value.astype(jnp.bfloat16)
                lower = (value - high.astype(jnp.float32)).astype(jnp.bfloat16)
                factor[slot, pl.ds(place + low, 16), 0:PB] = high
                factor[slot, pl.ds(place + low, 16), PB : 2 * PB] = lower
        moment[2, slot] = moment[1, slot]

    def second_product(code, slot):
        a = code >> 10
        sums = lax.dot_general(
            moment[2, slot], factor[slot], (((1,), (1,)), ((), ())), preferred_element_type=jnp.float32
        )
        total[a, 0] += sums[0:8, 0:PB]
        total[a, 1] += sums[0:8, PB : 2 * PB]

    def group(step):
        return [plan[(TOGETHER * step + slot) >> 7, (TOGETHER * step + slot) & 127] for slot in range(TOGETHER)]

    def stage(work, codes_now):
        for slot in range(TOGETHER):
            work(codes_now[slot], slot)

    def one_step(step, stages):
        made, multiplied, weighed = stages
        fresh = group(step)
        stage(second_product, weighed)
        stage(elementwise, multiplied)
        stage(first_product, made)
        stage(prepare, fresh)
        return fresh, made, multiplied

    one, two, three = group(0), group(1), group(2)
    stage(prepare, one)
    stage(first_product, one)
    stage(prepare, two)
    stage(elementwise, one)
    stage(first_product, two)
    stage(prepare, three)
    steps = jnp.maximum((number + TOGETHER - 1) // TOGETHER, 3)
    three, two, one = lax.fori_loop(3, steps, one_step, (three, two, one))
    stage(second_product, one)
    stage(elementwise, two)
    stage(first_product, three)
    stage(second_product, two)
    stage(elementwise, three)
    stage(second_product, three)
    length = length_ref[0]
    elapsed = step_ref[0].astype(jnp.float32) * length
    strength = BLAST_STRENGTH * jnp.exp(jnp.full((1, PB), -elapsed / DECAY_TIME, jnp.float32))
    for block in range(BLK_DEV):
        fields = all_ref[tile * CHUNK + 1 + block]
        columns = pl.ds(block * PB, PB)
        moments = total[block, 0, 0:4] + total[block, 0, 4:8]
        growth = -(total[block, 1, 0:1] + total[block, 1, 4:5])
        relative = fields[0:3] + 1.0
        spread_sq = jnp.sum(relative * relative, axis=0, keepdims=True) + 1.0
        source = strength * relative / (spread_sq * jnp.sqrt(spread_sq))
        pushed = (fields - centre[block])[0:3] * moments[0:1] - moments[1:4]
        forcing = pushed + source
        velocity = fields[3:6] + length * forcing
        position = fields[0:3] + length * velocity
        density = fields[6:7] + length * growth
        rates_ref[:, columns] = jnp.concatenate([growth, forcing], axis=0)
        ahead_ref[:, columns] = jnp.concatenate([position, velocity, density], axis=0)


def rates_of(step_index, time_step, gathered):
    smem = pl.BlockSpec(memory_space=pltpu.SMEM)
    vmem = pl.BlockSpec(memory_space=pltpu.VMEM)
    all_blocks, codes, centre, left, push, rho = gathered
    return pl.pallas_call(
        rates_kernel,
        out_shape=(
            jax.ShapeDtypeStruct((4, BLK_DEV * PB), jnp.float32),
            jax.ShapeDtypeStruct((7, BLK_DEV * PB), jnp.float32),
        ),
        in_specs=[smem, smem, smem] + [vmem] * 5,
        out_specs=(vmem, vmem),
        scratch_shapes=[
            pltpu.VMEM((BLK_DEV + 1, 2, 8, PB), jnp.float32),
            pltpu.VMEM((TOGETHER, 64, 2 * PB), jnp.bfloat16),
            pltpu.VMEM((TOGETHER, PB, 2 * PB), jnp.float32),
            pltpu.VMEM((TOGETHER, 2 * PB, 2 * PB), jnp.bfloat16),
            pltpu.VMEM((3, TOGETHER, 16, 2 * PB), jnp.bfloat16),
            pltpu.VMEM((2, TOGETHER, 8, PB), jnp.float32),
        ],
        compiler_params=pltpu.CompilerParams(vmem_limit_bytes=16 * 2**20),
        name="tile_rates",
    )(step_index, time_step, codes, all_blocks, centre, left, push, rho)


def on_device(particles, halo_up, halo_down, tile_first, tile_second, tile_live, step_index, time_step):
    mine = jnp.transpose(particles.reshape(8, BLK_DEV, PB), (1, 0, 2))
    gathered = gather(halo_up, halo_down, tile_first, tile_second, tile_live, mine)
    return rates_of(step_index, time_step, gathered)


def solution(mesh):
    placed = (
        P(None, ("slab", "tile")),
        P(("slab", "tile")),
        P(("slab", "tile")),
        P("slab", "tile"),
        P("slab", "tile"),
        P("slab", "tile"),
        P(),
        P(),
    )
    return jax.shard_map(
        on_device,
        mesh=mesh,
        in_specs=placed,
        out_specs=(P(None, ("slab", "tile")), P(None, ("slab", "tile"))),
        check_vma=False,
    )
```

```python
import heapq
import itertools

import jax
import jax.numpy as jnp
from jax import lax
from jax.experimental import pallas as pl
from jax.experimental.pallas import tpu as pltpu
from jax.sharding import PartitionSpec as P

PB = 128
BLK_DEV = 16
N_SLAB = 16
X, Z = 4, 8
N_TILE = X * Z
CHUNK = 1 + BLK_DEV + 2
NO_TILE = BLK_DEV * 1024

SMOOTHING = 1.0
KERNEL_NORM = 21.0 / (16.0 * 3.141592653589793)
SOUND_SPEED = 10.0
STIFFNESS = SOUND_SPEED * SOUND_SPEED / 7.0
VISCOSITY = 0.1
BLAST_STRENGTH = 8.0
DECAY_TIME = 8.0

MESH = pl.DeviceIdType.MESH

PARTS = (
    dict(first="x", x2="-", z4="-", lo=13, hi=19, at=1.9),
    dict(first="z", x2="-", z4="+", lo=7, hi=13, at=0.1),
    dict(first="z", x2="+", z4="-", lo=0, hi=7, at=0.4),
)
BLOCK_US = 4096 / 46.5e3
HOP_US = 3.0


def tree(part):
    x_from = {1: (0, "x+"), 3: (0, "x-"), 2: (1, "x+") if part["x2"] == "+" else (3, "x-")}
    z_from = {1: (0, "z+"), 2: (1, "z+"), 3: (2, "z+"), 7: (0, "z-"), 6: (7, "z-"), 5: (6, "z-")}
    z_from[4] = (3, "z+") if part["z4"] == "+" else (5, "z-")
    children = {}
    for dx, dz in itertools.product(range(X), range(Z)):
        if (dx, dz) == (0, 0):
            continue
        along_z = dz != 0 if part["first"] == "x" else dx == 0
        if along_z:
            parent, way = (dx, z_from[dz][0]), z_from[dz][1]
        else:
            parent, way = (x_from[dx][0], dz), x_from[dx][1]
        children.setdefault(parent, []).append((way, (dx, dz)))
    return children


def schedule():
    trees = [tree(part) for part in PARTS]

    def depth(index, node):
        return max([0] + [1 + depth(index, child) for _, child in trees[index].get(node, [])])

    free = {"x+": 0.0, "x-": 0.0, "z+": 0.0, "z-": 0.0}
    ticket = itertools.count()
    events = [(part["at"], next(ticket), index, (0, 0)) for index, part in enumerate(PARTS)]
    heapq.heapify(events)
    steps = []
    while events:
        now, _, index, node = heapq.heappop(events)
        sends = sorted(trees[index].get(node, []), key=lambda item: -depth(index, item[1]))
        steps.append((index, node, sends))
        blocks = PARTS[index]["hi"] - PARTS[index]["lo"]
        for way, child in sends:
            done = max(now, free[way]) + blocks * BLOCK_US
            free[way] = done
            heapq.heappush(events, (done + HOP_US, next(ticket), index, child))
    return steps


STEPS = schedule()
LEAVES = {(index, node) for index, node, sends in STEPS if not sends}
EARLY = 8


def gather_kernel(up_ref, down_ref, first_ref, second_ref, live_ref, mine_ref,
                  all_ref, codes_ref, centre_ref, left_ref, push_ref, rho_ref,
                  own, rim, slots, fetch_sem, rim_send, rim_recv, send_sem, recv_sem, leaf_sem):
    slab = lax.axis_index("slab")
    tile = lax.axis_index("tile")
    x, z = tile // Z, tile % Z
    above = lax.rem(slab + 1, N_SLAB)
    below = lax.rem(slab + N_SLAB - 1, N_SLAB)
    beside = {
        "x+": lax.rem(x + 1, X) * Z + z,
        "x-": lax.rem(x + X - 1, X) * Z + z,
        "z+": x * Z + lax.rem(z + 1, Z),
        "z-": x * Z + lax.rem(z + Z - 1, Z),
    }
    row = iota((8, PB), 0)

    def held(origin, low, high):
        return all_ref.at[pl.ds(origin * CHUNK + low, high - low)]

    place = pltpu.make_async_copy(mine_ref, held(tile, 1, 1 + BLK_DEV), fetch_sem.at[0])
    load = pltpu.make_async_copy(mine_ref, own, fetch_sem.at[1])
    fetch = [
        pltpu.make_async_copy(ref, slots.at[index], fetch_sem.at[2 + index])
        for index, ref in enumerate((first_ref, second_ref, live_ref))
    ]
    barrier = pltpu.get_barrier_semaphore()
    for way in beside:
        pl.semaphore_signal(barrier, inc=1, device_id=(slab, beside[way]), device_id_type=MESH)
    pl.semaphore_signal(barrier, inc=1, device_id=(above, tile), device_id_type=MESH)
    pl.semaphore_signal(barrier, inc=1, device_id=(below, tile), device_id_type=MESH)
    place.start()
    for copy in fetch:
        copy.start()
    load.start()
    pl.semaphore_wait(barrier, 6)

    def rim_copy(side):
        return pltpu.make_async_remote_copy(
            src_ref=rim.at[pl.ds(side, 1)],
            dst_ref=held(tile, 1 + BLK_DEV + side, 2 + BLK_DEV + side),
            send_sem=rim_send.at[side],
            recv_sem=rim_recv.at[side],
            device_id=(above if side == 0 else below, tile),
            device_id_type=MESH,
        )

    def pass_on(where, signal, way, source=None):
        return pltpu.make_async_remote_copy(
            src_ref=where if source is None else source,
            dst_ref=where,
            send_sem=send_sem,
            recv_sem=signal,
            device_id=(slab, beside[way]),
            device_id_type=MESH,
        )

    from_x = [lax.rem(x + X - step, X) * (Z * CHUNK) for step in range(X)]
    from_z = [lax.rem(z + Z - step, Z) * CHUNK for step in range(Z)]

    def piece(index, node):
        low, high = PARTS[index]["lo"], PARTS[index]["hi"]
        return all_ref.at[pl.ds(from_x[node[0]] + from_z[node[1]] + low, high - low)]

    def arrival(index, node):
        if (index, node) in LEAVES:
            return leaf_sem.at[0 if PARTS[index]["lo"] == 0 else 1]
        return recv_sem.at[index * N_TILE + node[0] * Z + node[1]]

    def one_pair(pair, carry):
        for block in (2 * pair, 2 * pair + 1):
            middle, side = receiver(own[block], row)
            centre_ref[block] = middle
            left_ref[block] = side.astype(jnp.bfloat16)
            push_ref[block] = jnp.broadcast_to(side[:, 56:57], (PB, PB))
            rho_ref[block] = jnp.broadcast_to(side[:, 57:58], (PB, PB))
        return carry

    rims = [rim_copy(0), rim_copy(1)]
    for index, node, sends in STEPS:
        part = PARTS[index]
        if node == (0, 0) and part["lo"] > 0 and part["hi"] <= 1 + BLK_DEV:
            for way, child in sends:
                source = mine_ref.at[pl.ds(part["lo"] - 1, part["hi"] - part["lo"])]
                pass_on(piece(index, node), arrival(index, child), way, source).start()
    for copy in fetch:
        copy.wait()
    all_ref[tile * CHUNK] = jnp.where(
        row == 0, slots[0], jnp.where(row == 1, slots[1], jnp.where(row == 2, slots[2], 0))
    ).astype(jnp.float32)
    load.wait()
    rim[0] = own[up_ref[0]]
    rim[1] = own[down_ref[0]]
    lax.fori_loop(0, 1, one_pair, 0)
    for copy in rims:
        copy.start()
    place.wait()
    for index, node, sends in STEPS:
        if (index, node) in LEAVES:
            continue
        part = PARTS[index]
        if node == (0, 0) and part["lo"] > 0 and part["hi"] <= 1 + BLK_DEV:
            continue
        where = piece(index, node)
        if node != (0, 0):
            pass_on(where, arrival(index, node), "x+").wait_recv()
        elif part["hi"] == CHUNK:
            lax.fori_loop(1, EARLY // 2, one_pair, 0)
            for copy in rims:
                copy.wait_recv()
        for way, child in sends:
            pass_on(where, arrival(index, child), way).start()
    lax.fori_loop(EARLY // 2, BLK_DEV // 2, one_pair, 0)
    centre_ref[BLK_DEV] = jnp.zeros((8, PB), jnp.float32)
    left_ref[BLK_DEV] = jnp.zeros((PB, 64), jnp.bfloat16)
    push_ref[BLK_DEV] = jnp.zeros((PB, PB), jnp.float32)
    rho_ref[BLK_DEV] = jnp.full((PB, PB), -1.0, jnp.float32)
    listed, other = (sum(PARTS[index]["hi"] - PARTS[index]["lo"] for index, _ in LEAVES
                         if (PARTS[index]["lo"] == 0) == first) for first in (True, False))
    pass_on(all_ref.at[pl.ds(0, listed)], leaf_sem.at[0], "x+").wait_recv()
    codes_ref[...] = choose_tiles(all_ref, slab, tile)
    pass_on(all_ref.at[pl.ds(0, other)], leaf_sem.at[1], "x+").wait_recv()
    for copy in rims:
        copy.wait_send()
    pass_on(all_ref.at[pl.ds(0, (N_TILE - 1) * CHUNK)], leaf_sem.at[0], "x+").wait_send()


def gather(halo_up, halo_down, tile_first, tile_second, tile_live, mine):
    smem = pl.BlockSpec(memory_space=pltpu.SMEM)
    hbm = pl.BlockSpec(memory_space=pltpu.HBM)
    vmem = pl.BlockSpec(memory_space=pltpu.VMEM)
    in_hbm = [
        pltpu.with_memory_space_constraint(array, pltpu.HBM)
        for array in (tile_first, tile_second, tile_live, mine)
    ]
    return pl.pallas_call(
        gather_kernel,
        out_shape=(
            jax.ShapeDtypeStruct((N_TILE * CHUNK, 8, PB), jnp.float32),
            jax.ShapeDtypeStruct((8, PB), jnp.int32),
            jax.ShapeDtypeStruct((BLK_DEV + 1, 8, PB), jnp.float32),
            jax.ShapeDtypeStruct((BLK_DEV + 1, PB, 64), jnp.bfloat16),
            jax.ShapeDtypeStruct((BLK_DEV + 1, PB, PB), jnp.float32),
            jax.ShapeDtypeStruct((BLK_DEV + 1, PB, PB), jnp.float32),
        ),
        in_specs=[smem, smem, hbm, hbm, hbm, hbm],
        out_specs=(vmem,) * 6,
        scratch_shapes=[
            pltpu.VMEM((BLK_DEV, 8, PB), jnp.float32),
            pltpu.VMEM((2, 8, PB), jnp.float32),
            pltpu.VMEM((3, 1, PB), jnp.int32),
            pltpu.SemaphoreType.DMA((5,)),
            pltpu.SemaphoreType.DMA((2,)),
            pltpu.SemaphoreType.DMA((2,)),
            pltpu.SemaphoreType.DMA,
            pltpu.SemaphoreType.DMA((len(PARTS) * N_TILE,)),
            pltpu.SemaphoreType.DMA((2,)),
        ],
        compiler_params=pltpu.CompilerParams(collective_id=0, has_side_effects=True, vmem_limit_bytes=16 * 2**20),
        name="gather_blocks",
    )(halo_up, halo_down, *in_hbm)


def iota(shape, axis):
    return lax.broadcasted_iota(jnp.int32, shape, axis)


def choose_tiles(all_ref, slab, tile):
    first, second, live = (
        jnp.concatenate(
            [all_ref[origin * CHUNK, pl.ds(place, 1)] for origin in range(N_TILE)], axis=0
        ).astype(jnp.int32)
        for place in range(3)
    )
    missing = ((slab == 0) & (second >= 512) & (second < 544)) | ((slab == N_SLAB - 1) & (second >= 544))
    wanted = ((first >> 4) == tile) & (live == 1) & jnp.logical_not(missing)
    source = jnp.where(
        second < 512,
        (second >> 4) * CHUNK + 1 + (second & 15),
        ((second - 512) & 31) * CHUNK + 1 + BLK_DEV + ((second - 512) >> 5),
    )
    code = ((first & 15) * 1024 + source).astype(jnp.float32)
    ones = jnp.where(wanted, 1.0, 0.0)
    upto = (iota((PB, PB), 0) <= iota((PB, PB), 1)).astype(jnp.float32)
    within = jnp.dot(ones, upto, preferred_element_type=jnp.float32)
    earlier = (iota((N_TILE, N_TILE), 1) < iota((N_TILE, N_TILE), 0)).astype(jnp.float32)
    before = jnp.dot(earlier, within, preferred_element_type=jnp.float32)[:, PB - 1 :]
    place = jnp.where(wanted, (before + within).astype(jnp.int32) - 1, -1)
    target = iota((PB, PB), 0)
    chosen = jnp.zeros((PB, PB), jnp.float32)
    for row in range(N_TILE):
        chosen = jnp.where(place[row : row + 1, :] == target, code[row : row + 1, :], chosen)
    codes = lax.dot_general(
        jnp.ones((8, PB), jnp.float32), chosen, (((1,), (1,)), ((), ())),
        precision=lax.Precision.HIGHEST, preferred_element_type=jnp.float32,
    )
    count = jnp.sum(before[N_TILE - 1 :, :] + within[N_TILE - 1 :, PB - 1 :])
    row = iota((8, PB), 0)
    codes = jnp.where((row == 0) & (iota((8, PB), 1).astype(jnp.float32) < count), codes, float(NO_TILE))
    return jnp.where(row == 2, count, codes).astype(jnp.int32)


def shifted(rows, up):
    return pltpu.roll(rows, (8 - up) % 8, 0)


def parts_of(value):
    high = value.astype(jnp.bfloat16).astype(jnp.float32)
    rest = value - high
    middle = rest.astype(jnp.bfloat16).astype(jnp.float32)
    return high, middle, rest - middle


def squares_and_products(centred):
    squares = centred * centred
    products = centred * shifted(centred, 3)
    return (
        squares + shifted(squares, 1) + shifted(squares, 2),
        products + shifted(products, 1) + shifted(products, 2),
    )


def pressure_term(density):
    squared = density * density
    return STIFFNESS * (squared * squared * squared * density - 1.0) / squared


def receiver(fields, row):
    centre = jnp.where(row < 6, jnp.broadcast_to(fields[:, 0:1], (8, PB)), 0.0)
    centred = fields - centre
    squares, products = squares_and_products(centred)
    plain = jnp.where(row < 6, centred, jnp.where(row == 6, 1.0, 0.0))
    high, middle, low = parts_of(plain)
    extra = jnp.zeros((8, PB), jnp.float32)
    for place, value in enumerate(parts_of(squares) + parts_of(products)):
        extra = jnp.where(row == place, value if place == 0 else shifted(value, 8 - place), extra)
    pressure = pressure_term(fields)
    columns = jnp.where(row == 0, shifted(pressure, 6), jnp.where(row == 1, shifted(-0.5 * fields, 5), 0.0))
    return centre, jnp.concatenate([high, high, middle, middle, high, low, extra, columns], axis=0).T


def actor_side(centred, row):
    squares, products = squares_and_products(centred)
    for_square = jnp.where(row < 3, -2.0 * centred, jnp.where(row == 6, shifted(squares, 2), 0.0))
    for_approach = jnp.where(
        row < 3, -shifted(centred, 3), jnp.where(row < 6, -shifted(centred, 5), jnp.where(row == 6, shifted(products, 2), 0.0))
    )
    sides = []
    for value, ones in ((for_square, row < 3), (for_approach, (row >= 3) & (row < 6))):
        high, middle, low = parts_of(value)
        extra = jnp.where(ones, 1.0, 0.0)
        sides.append(
            jnp.concatenate([high, middle, high, middle, low, high, extra, jnp.zeros((8, PB), jnp.float32)], axis=0)
        )
    return jnp.concatenate(sides, axis=1).astype(jnp.bfloat16)


TOGETHER = 3


def rates_kernel(step_ref, length_ref, codes, all_ref, centre, left, push, rho, rates_ref, ahead_ref,
                 total, right, squares, factor, moment, acts, plan, plan_sem):
    tile = lax.axis_index("tile")
    row = iota((8, PB), 0)
    copy = pltpu.make_async_copy(codes, plan, plan_sem)
    copy.start()
    total[...] = jnp.zeros_like(total)
    copy.wait()
    number = plan[2, 0]

    def prepare(code, slot):
        fields = all_ref[code & 1023]
        centred = fields - centre[code >> 10]
        right[slot] = actor_side(centred, row)
        mass = jnp.broadcast_to(fields[7:8] * (5.0 * KERNEL_NORM / 8.0), (8, PB))
        weighted = jnp.where(row == 0, 1.0, shifted(centred, 7)) * mass
        high = weighted.astype(jnp.bfloat16).astype(jnp.float32)
        both = jnp.where(row < 4, high, shifted(weighted - high, 4))
        both = jnp.concatenate([both, jnp.zeros((8, PB), jnp.float32)], axis=0).astype(jnp.bfloat16)
        moment[0, slot] = jnp.concatenate([both, both], axis=1)
        acts[0, slot] = jnp.where(row == 6, pressure_term(fields), -0.5 * shifted(fields, 7))

    def first_product(code, slot):
        squares[slot] = jnp.dot(left[code >> 10], right[slot], preferred_element_type=jnp.float32)
        moment[1, slot] = moment[0, slot]
        acts[1, slot] = acts[0, slot]

    def elementwise(code, slot):
        a = code >> 10
        act_push = jnp.broadcast_to(acts[1, slot, 6:7], (16, PB))
        act_rho = jnp.broadcast_to(acts[1, slot, 7:8], (16, PB))
        for low in range(0, PB, 16):
            rows = pl.ds(low, 16)
            dist_sq = jnp.maximum(squares[slot, rows, 0:PB], 1e-30)
            approach = squares[slot, rows, PB : 2 * PB]
            reach = jnp.maximum(2.0 - dist_sq * lax.rsqrt(dist_sq), 0.0)
            weight = reach * reach * reach
            growth = approach * weight
            damping = jnp.minimum(approach, 0.0) / ((dist_sq + 0.01) * (rho[a, rows] + act_rho))
            pressing = (push[a, rows] + act_push + damping) * weight
            for place, value in ((0, pressing), (PB, growth)):
                high = value.astype(jnp.bfloat16)
                lower = (value - high.astype(jnp.float32)).astype(jnp.bfloat16)
                factor[slot, pl.ds(place + low, 16), 0:PB] = high
                factor[slot, pl.ds(place + low, 16), PB : 2 * PB] = lower
        moment[2, slot] = moment[1, slot]

    def second_product(code, slot):
        a = code >> 10
        sums = lax.dot_general(
            moment[2, slot], factor[slot], (((1,), (1,)), ((), ())), preferred_element_type=jnp.float32
        )
        total[a, 0] += sums[0:8, 0:PB]
        total[a, 1] += sums[0:8, PB : 2 * PB]

    def group(step):
        return [plan[(TOGETHER * step + slot) >> 7, (TOGETHER * step + slot) & 127] for slot in range(TOGETHER)]

    def stage(work, codes_now):
        for slot in range(TOGETHER):
            work(codes_now[slot], slot)

    def one_step(step, stages):
        made, multiplied, weighed = stages
        fresh = group(step)
        stage(second_product, weighed)
        stage(elementwise, multiplied)
        stage(first_product, made)
        stage(prepare, fresh)
        return fresh, made, multiplied

    one, two, three = group(0), group(1), group(2)
    stage(prepare, one)
    stage(first_product, one)
    stage(prepare, two)
    stage(elementwise, one)
    stage(first_product, two)
    stage(prepare, three)
    steps = jnp.maximum((number + TOGETHER - 1) // TOGETHER, 3)
    three, two, one = lax.fori_loop(3, steps, one_step, (three, two, one))
    stage(second_product, one)
    stage(elementwise, two)
    stage(first_product, three)
    stage(second_product, two)
    stage(elementwise, three)
    stage(second_product, three)
    length = length_ref[0]
    elapsed = step_ref[0].astype(jnp.float32) * length
    strength = BLAST_STRENGTH * jnp.exp(jnp.full((1, PB), -elapsed / DECAY_TIME, jnp.float32))
    for block in range(BLK_DEV):
        fields = all_ref[tile * CHUNK + 1 + block]
        columns = pl.ds(block * PB, PB)
        moments = total[block, 0, 0:4] + total[block, 0, 4:8]
        growth = -(total[block, 1, 0:1] + total[block, 1, 4:5])
        relative = fields[0:3] + 1.0
        spread_sq = jnp.sum(relative * relative, axis=0, keepdims=True) + 1.0
        source = strength * relative / (spread_sq * jnp.sqrt(spread_sq))
        pushed = (fields - centre[block])[0:3] * moments[0:1] - moments[1:4]
        forcing = pushed + source
        velocity = fields[3:6] + length * forcing
        position = fields[0:3] + length * velocity
        density = fields[6:7] + length * growth
        rates_ref[:, columns] = jnp.concatenate([growth, forcing], axis=0)
        ahead_ref[:, columns] = jnp.concatenate([position, velocity, density], axis=0)


def rates_of(step_index, time_step, gathered):
    smem = pl.BlockSpec(memory_space=pltpu.SMEM)
    vmem = pl.BlockSpec(memory_space=pltpu.VMEM)
    all_blocks, codes, centre, left, push, rho = gathered
    return pl.pallas_call(
        rates_kernel,
        out_shape=(
            jax.ShapeDtypeStruct((4, BLK_DEV * PB), jnp.float32),
            jax.ShapeDtypeStruct((7, BLK_DEV * PB), jnp.float32),
        ),
        in_specs=[smem, smem] + [vmem] * 6,
        out_specs=(vmem, vmem),
        scratch_shapes=[
            pltpu.VMEM((BLK_DEV + 1, 2, 8, PB), jnp.float32),
            pltpu.VMEM((TOGETHER, 64, 2 * PB), jnp.bfloat16),
            pltpu.VMEM((TOGETHER, PB, 2 * PB), jnp.float32),
            pltpu.VMEM((TOGETHER, 2 * PB, 2 * PB), jnp.bfloat16),
            pltpu.VMEM((3, TOGETHER, 16, 2 * PB), jnp.bfloat16),
            pltpu.VMEM((2, TOGETHER, 8, PB), jnp.float32),
            pltpu.SMEM((8, PB), jnp.int32),
            pltpu.SemaphoreType.DMA,
        ],
        compiler_params=pltpu.CompilerParams(vmem_limit_bytes=16 * 2**20),
        name="tile_rates",
    )(step_index, time_step, codes, all_blocks, centre, left, push, rho)


def on_device(particles, halo_up, halo_down, tile_first, tile_second, tile_live, step_index, time_step):
    mine = jnp.transpose(particles.reshape(8, BLK_DEV, PB), (1, 0, 2))
    gathered = gather(halo_up, halo_down, tile_first, tile_second, tile_live, mine)
    return rates_of(step_index, time_step, gathered)


def solution(mesh):
    placed = (
        P(None, ("slab", "tile")),
        P(("slab", "tile")),
        P(("slab", "tile")),
        P("slab", "tile"),
        P("slab", "tile"),
        P("slab", "tile"),
        P(),
        P(),
    )
    return jax.shard_map(
        on_device,
        mesh=mesh,
        in_specs=placed,
        out_specs=(P(None, ("slab", "tile")), P(None, ("slab", "tile"))),
        check_vma=False,
    )
```
